512 devices in a mesh: rows: 32 (over x, z), cols: 16 (over y, core).
Axes of the slice: x: 4, y: 8, z: 8, core: 2. Of those that a mesh axis runs over, the one named last changes fastest.
Arguments:
- targets: float32 [3, 65536], P(None, 'rows'), may hold values from 0 to 1
- sources: float32 [3, 65536], P(None, 'cols'), may hold values from 0 to 1
- weights: float32 [65536], P('cols'), may hold values from 0.5 to 2
- counts: int32 [4096], P('cols'), may hold values from 8 to 16, as said below
- omega: bfloat16 [65536, 128], P('cols'), may hold values from -0.0234375 to 0.0234375
Outputs:
- basis: float32 [65536, 128], P('rows')
- projected: float32 [65536, 128], P(('cols', 'rows'))
The draws below stay inside these ranges and needn't reach their ends.
Inputs may be any that keep to these rules, and one draw needn't show every extreme that they name: `counts`: some panel uses all 16 nodes.
All inputs are finite; a program needn't handle non-finite values.
Results may differ from the reference program's by a relative error of at most 0.0033.
Values may be sent and summed in bfloat16 or wider, within the bound.
No kernel may reach another device: no remote copies, remote signals or barrier semaphores. Data moves between devices by JAX's collectives and lax.ppermute only.
A program may use at most 64 MiB of HBM per device.

```python
import math
import jax
import jax.numpy as jnp
from jax import lax

RANK = 128
PANEL = 16
M = 65536
N = 65536


def draw_counts(key, part):
    drawn = jax.random.randint(key, (N // PANEL,), PANEL // 2, PANEL + 1)
    chosen_panel = jax.random.randint(jax.random.fold_in(key, 7), (), 0, N // PANEL)
    return drawn.at[chosen_panel].set(PANEL).astype(jnp.int32)


def steps_of(stream_key, extent, split, smallest, high):
    loudness, own = 1.0, jax.random.fold_in(stream_key, 6)
    for axis_at, shards_of in split:
        steps = jnp.exp(jax.random.uniform(jax.random.fold_in(own, axis_at), (shards_of,), jnp.float32, smallest / len(split), high / len(split)))
        loudness = loudness * jnp.repeat(steps, extent[axis_at] // shards_of).reshape([-1 if axis == axis_at else 1 for axis in range(len(extent))])
    return loudness


def scatter_about(rng, shape, deviation, limit, cuts=(), kind=jnp.bfloat16):
    values = jax.random.normal(rng, shape, jnp.float32) * deviation
    if len(cuts) > 0:
        values = steps_of(rng, shape, cuts, -0.22, 0.18) * values
    return jnp.clip(values, min=-limit, max=limit).astype(kind)


def setup_inputs(seed: int = 0) -> dict:
    key_list = jax.random.split(jax.random.key(seed), 6)
    return {
        "targets": jnp.clip(1.0 * jax.random.uniform(key_list[0], (3, M), jnp.float32) ** steps_of(key_list[0], (3, M), ((1, 32),), -0.2, 0.2), 0.0, 1.0),
        "sources": jnp.clip(1.0 * jax.random.uniform(key_list[1], (3, N), jnp.float32) ** steps_of(key_list[1], (3, N), ((1, 16),), -0.2, 0.2), 0.0, 1.0),
        "weights": jnp.clip(jnp.exp(math.log(2.0) - 1.3862944 * jax.random.uniform(key_list[2], (N,), jnp.float32) ** steps_of(key_list[2], (N,), ((0, 16),), -0.2, 0.2)), 0.5, 2.0),
        "counts": draw_counts(jax.random.fold_in(key_list[5], 71), 0),
        "omega": scatter_about(key_list[4], (N, RANK), N ** -0.5, 0.0234375, ((0, 16),)),
    }


wave_number = 160.0
separation = 2.0

def kernel_cols(targets, src_block, wts_block):
    diff_x = targets[0][None, :] - (src_block[0][:, None] + separation)
    diff_y = targets[1][None, :] - src_block[1][:, None]
    diff_z = targets[2][None, :] - src_block[2][:, None]
    distance = jnp.sqrt(diff_x * diff_x + diff_y * diff_y + diff_z * diff_z)
    return (wts_block[:, None] * jnp.cos(wave_number * distance) / distance).astype(jnp.bfloat16)

def reference(targets, sources, weights, counts, omega):
    node_index = jnp.arange(N, dtype=jnp.int32)
    usable = (node_index % PANEL < jnp.repeat(counts, PANEL)).astype(jnp.float32)
    node_weight = weights * usable
    block_width = math.gcd(N, 512)
    nblocks = N // block_width
    src_blocks = sources.reshape(3, nblocks, block_width).transpose(1, 0, 2)
    wts_blocks = node_weight.reshape(nblocks, block_width)
    omega_blocks = omega.reshape(nblocks, block_width, RANK)

    def sketch_turn(total, inputs):
        kernel_tile = kernel_cols(targets, inputs[0], inputs[1])
        return (total + lax.dot_general(kernel_tile.astype(jnp.float32), inputs[2].astype(jnp.float32), (((0,), (0,)), ((), ())), preferred_element_type=jnp.float32), None)
    sketch, _ = lax.scan(sketch_turn, jnp.zeros((M, RANK), jnp.float32), (src_blocks, wts_blocks, omega_blocks))
    gram_matrix = jnp.dot(sketch.T.astype(jnp.float32), sketch.astype(jnp.float32), precision=lax.Precision.HIGHEST, preferred_element_type=jnp.float32)
    lower_factor = jnp.linalg.cholesky(gram_matrix)
    ortho = lax.linalg.triangular_solve(lower_factor, sketch, left_side=False, lower=True, transpose_a=True)
    ortho_low = ortho.astype(jnp.bfloat16)

    def project_turn(carry, inputs):
        kernel_tile = kernel_cols(targets, inputs[0], inputs[1])
        return (carry, jnp.dot(kernel_tile.astype(jnp.float32), ortho_low.astype(jnp.float32), preferred_element_type=jnp.float32))
    _, projected = lax.scan(project_turn, jnp.zeros((), jnp.float32), (src_blocks, wts_blocks))
    return (ortho * math.sqrt(M), projected.reshape(N, RANK))
```

```python
import functools
import math

import jax
import jax.numpy as jnp
from jax import lax
from jax.experimental import pallas as pl
from jax.experimental.pallas import tpu as pltpu
from jax.sharding import PartitionSpec as P

f32 = jnp.float32
bf16 = jnp.bfloat16
wave_number = 160.0
separation = 2.0
turns = wave_number / (2.0 * math.pi)
sine = (6.283164043875678, -41.33714231633244, 81.34076713243772, -70.99341720807224)
target_tile = 256
source_tile = 512


def thirds(values):
    high = values.astype(bf16)
    rest = values - high.astype(f32)
    middle = rest.astype(bf16)
    low = (rest - middle.astype(f32)).astype(bf16)
    return high, middle, low


def pick_rows(rows, shape):
    at = lax.broadcasted_iota(jnp.int32, shape, 0)
    out = jnp.zeros(shape, f32)
    for k, row in enumerate(rows):
        out = jnp.where(at == k, jnp.broadcast_to(row, shape), out)
    return out


def put_thirds(ref, values, outer):
    parts = [part.astype(f32) for part in thirds(values)]
    for p in range(3):
        for q in range(3):
            k = 3 * p + q
            ref[8 * k : 8 * k + 8, :] = parts[p if outer else q]


def sketch_kernel(targets, sources, weights, usable, omega, tiles, sketch,
                  feature, tfeat, afeat, bfeat, masked, a_buf, b_buf, acc):
    step = pl.program_id(0)
    ncols = sources.shape[1]
    turns_n = ncols // source_tile

    @pl.when(step == 0)
    def _():
        nrows = targets.shape[1]
        feature[...] = jnp.zeros_like(feature)
        tx = (targets[0:1, :] - (0.5 + 0.5 * separation)) * turns
        ty = (targets[1:2, :] - 0.5) * turns
        tz = (targets[2:3, :] - 0.5) * turns
        rows = [tx, ty, tz, tx * tx + ty * ty + tz * tz, jnp.ones_like(tx)]
        view = feature.at[:, 0:nrows]
        put_thirds(view, pick_rows(rows, (8, nrows)), True)
        for k in range(nrows // 128):
            tfeat[128 * k : 128 * k + 128, :] = feature[:, 128 * k : 128 * k + 128].T.astype(bf16)
        sx = (sources[0:1, :] + (0.5 * separation - 0.5)) * turns
        sy = (sources[1:2, :] - 0.5) * turns
        sz = (sources[2:3, :] - 0.5) * turns
        norm = sx * sx + sy * sy + sz * sz
        inverse = 1.0 / weights[...]
        for ref, scale in ((bfeat, inverse), (afeat, inverse * inverse)):
            rows = [-2.0 * sx * scale, -2.0 * sy * scale, -2.0 * sz * scale, scale, norm * scale]
            put_thirds(feature, pick_rows(rows, (8, ncols)), False)
            ref[...] = feature[...].astype(bf16)
        flag = pick_rows([usable[...]], (8, ncols)).astype(bf16)
        column = lax.dot_general(
            flag, jnp.ones((8, omega.shape[1]), bf16), (((0,), (0,)), ((), ())), preferred_element_type=f32
        )
        masked[...] = (omega[...].astype(f32) * column).astype(bf16)

    here = tfeat[pl.ds(pl.multiple_of(step * target_tile, target_tile), target_tile), :]

    def cols(j):
        return pl.ds(pl.multiple_of(j * source_tile, source_tile), source_tile)

    def distances(j):
        slot = lax.rem(j, 2)
        a_buf[slot] = jnp.dot(here, afeat[:, cols(j)], preferred_element_type=f32)
        b_buf[slot] = jnp.dot(here, bfeat[:, cols(j)], preferred_element_type=f32)

    def evaluate(j):
        slot = lax.rem(j, 2)
        for r in range(0, target_tile, 16):
            a = a_buf[slot, r : r + 16, :]
            b = b_buf[slot, r : r + 16, :]
            over = lax.rsqrt(a)
            turn = b * over
            away = 0.25 - jnp.abs(turn - jnp.round(turn))
            square = away * away
            c0, c1, c2, c3 = (turns * c for c in sine)
            wave = ((c3 * square + c2) * square + c1) * square + c0
            tiles[r : r + 16, cols(j)] = ((wave * away) * over).astype(bf16)

    def accumulate(j):
        acc[...] += jnp.dot(tiles[:, cols(j)], masked[cols(j), :], preferred_element_type=f32)

    acc[...] = jnp.zeros_like(acc)
    distances(0)
    distances(1)
    evaluate(0)

    def turn(j, carry):
        distances(lax.rem(j + 1, turns_n))
        evaluate(j)
        accumulate(j - 1)
        return carry

    lax.fori_loop(1, turns_n, turn, 0)
    accumulate(turns_n - 1)
    sketch[...] = acc[...].astype(bf16)


def make_sketch(targets, sources, weights, usable, omega):
    nrows, ncols, rank = targets.shape[1], sources.shape[1], omega.shape[1]
    whole = lambda i: (0, 0)
    once = dict(pipeline_mode=pl.Buffered(1))
    return pl.pallas_call(
        sketch_kernel,
        grid=(nrows // target_tile,),
        in_specs=[
            pl.BlockSpec((3, nrows), whole, **once),
            pl.BlockSpec((3, ncols), whole, **once),
            pl.BlockSpec((1, ncols), whole, **once),
            pl.BlockSpec((1, ncols), whole, **once),
            pl.BlockSpec((ncols, rank), whole, **once),
        ],
        out_specs=[
            pl.BlockSpec((target_tile, ncols), lambda i: (i, 0)),
            pl.BlockSpec((target_tile, rank), lambda i: (i, 0)),
        ],
        out_shape=[
            jax.ShapeDtypeStruct((nrows, ncols), bf16),
            jax.ShapeDtypeStruct((nrows, rank), bf16),
        ],
        scratch_shapes=[
            pltpu.VMEM((128, ncols), f32),
            pltpu.VMEM((nrows, 128), bf16),
            pltpu.VMEM((128, ncols), bf16),
            pltpu.VMEM((128, ncols), bf16),
            pltpu.VMEM((ncols, rank), bf16),
            pltpu.VMEM((2, target_tile, source_tile), f32),
            pltpu.VMEM((2, target_tile, source_tile), f32),
            pltpu.VMEM((target_tile, rank), f32),
        ],
        name="sketch",
    )(targets, sources, weights, usable, omega)


def piece_kernel(parts, out):
    total = parts[0].astype(f32)
    for k in range(1, parts.shape[0]):
        total += parts[k].astype(f32)
    low = total.astype(bf16)
    for k in range(out.shape[0]):
        out[k] = low


def add_pieces(parts):
    return pl.pallas_call(
        piece_kernel, out_shape=jax.ShapeDtypeStruct(parts.shape, bf16), name="pieces"
    )(parts)


def project_kernel(sketch, tiles, usable, out, flipped, gram):
    rank = sketch.shape[1]
    band = gram.shape[0] // lax.axis_size("cols")

    @pl.when(pl.program_id(0) == 0)
    def _():
        flipped[...] = sketch[...].astype(f32).T.astype(bf16)
        gram[...] = jnp.dot(flipped[...], sketch[...], preferred_element_type=f32)

    product = jnp.dot(flipped[...], tiles[...], preferred_element_type=f32)
    product = (product * usable[...]).astype(bf16)
    first = pl.multiple_of(lax.axis_index("cols") * band, band)
    own = jnp.concatenate([part.astype(f32) for part in thirds(gram[pl.ds(first, band), :])], axis=0)
    own = jnp.concatenate([own, jnp.zeros((32 - 3 * band, rank), f32)], axis=0).astype(bf16)
    for k in range(out.shape[0]):
        out[k, 0:rank, :] = product[:, 128 * k : 128 * k + 128]
        out[k, rank : rank + 32, :] = own


def project(sketch, tiles, usable, row_devices):
    nrows, ncols = tiles.shape
    rank = sketch.shape[1]
    width = 512
    dests = width // (ncols // row_devices)
    return pl.pallas_call(
        project_kernel,
        grid=(ncols // width,),
        in_specs=[
            pl.BlockSpec((nrows, rank), lambda j: (0, 0), pipeline_mode=pl.Buffered(1)),
            pl.BlockSpec((nrows, width), lambda j: (0, j)),
            pl.BlockSpec((1, width), lambda j: (0, j)),
        ],
        out_specs=pl.BlockSpec((dests, rank + 32, 128), lambda j: (j, 0, 0)),
        out_shape=jax.ShapeDtypeStruct((row_devices, rank + 32, 128), bf16),
        scratch_shapes=[pltpu.VMEM((rank, nrows), bf16), pltpu.VMEM((rank, rank), f32)],
        name="project",
    )(sketch, tiles, usable)


def fold_kernel(parts, product, band):
    total = parts[0].astype(f32)
    for k in range(1, parts.shape[0]):
        total += parts[k].astype(f32)
    rank = product.shape[0]
    rows = band.shape[1]
    product[...] = total[0:rank]
    own = total[rank : rank + rows] + (
        total[rank + rows : rank + 2 * rows] + total[rank + 2 * rows : rank + 3 * rows]
    )
    for k in range(band.shape[0]):
        band[k] = own


def fold(parts, col_devices):
    rank = parts.shape[1] - 32
    return pl.pallas_call(
        fold_kernel,
        out_shape=[
            jax.ShapeDtypeStruct((rank, rank), f32),
            jax.ShapeDtypeStruct((col_devices, rank // col_devices, rank), f32),
        ],
        name="fold",
    )(parts)


def finish_kernel(scale, sketch, product, inverse, basis, projected):
    high, middle, low = thirds(inverse[...] * scale)
    contract = (((1,), (1,)), ((), ()))
    rows = sketch[...]
    total = lax.dot_general(rows, low, contract, preferred_element_type=f32)
    total += lax.dot_general(rows, middle, contract, preferred_element_type=f32)
    basis[...] = total + lax.dot_general(rows, high, contract, preferred_element_type=f32)
    projected[...] = lax.dot_general(
        product[...].T,
        inverse[...],
        contract,
        precision=lax.Precision.HIGHEST,
        preferred_element_type=f32,
    )


def finish(sketch, product, inverse, scale):
    return pl.pallas_call(
        functools.partial(finish_kernel, scale),
        out_shape=[
            jax.ShapeDtypeStruct(sketch.shape, f32),
            jax.ShapeDtypeStruct(product.shape, f32),
        ],
        name="finish",
    )(sketch, product, inverse)


def shards(targets, sources, weights, counts, omega):
    rows_here, cols_here, rank = targets.shape[1], sources.shape[1], omega.shape[1]
    row_devices, col_devices = lax.axis_size("rows"), lax.axis_size("cols")
    panel_count = counts.shape[0]
    usable = (
        (lax.broadcasted_iota(jnp.int32, (panel_count, cols_here // panel_count), 1) < counts[:, None])
        .reshape(1, cols_here)
        .astype(f32)
    )
    tiles, partial = make_sketch(targets, sources, weights.reshape(1, cols_here), usable, omega)
    pieces = lax.all_to_all(partial.reshape(col_devices, -1, rank), "cols", 0, 0)
    sketch = lax.all_to_all(add_pieces(pieces), "cols", 0, 0).reshape(rows_here, rank)
    terms = lax.all_to_all(project(sketch, tiles, usable, row_devices), "rows", 0, 0)
    product, band = fold(terms, col_devices)
    gram_matrix = lax.all_to_all(band, "cols", 0, 0).reshape(rank, rank)
    lower_factor = jnp.linalg.cholesky(gram_matrix)
    inverse = lax.linalg.triangular_solve(lower_factor, jnp.eye(rank, dtype=f32), left_side=True, lower=True)
    return finish(sketch, product, inverse, math.sqrt(rows_here * row_devices))


def solution(mesh):
    return jax.shard_map(
        shards,
        mesh=mesh,
        in_specs=(P(None, "rows"), P(None, "cols"), P("cols"), P("cols"), P("cols", None)),
        out_specs=(P("rows", None), P(("cols", "rows"), None)),
        check_vma=False,
    )
```

```python
import functools
import math

import jax
import jax.numpy as jnp
from jax import lax
from jax.experimental import pallas as pl
from jax.experimental.pallas import tpu as pltpu
from jax.sharding import PartitionSpec as P

f32 = jnp.float32
bf16 = jnp.bfloat16
wave_number = 160.0
separation = 2.0
turns = wave_number / (2.0 * math.pi)
sine = (6.283164043875678, -41.33714231633244, 81.34076713243772, -70.99341720807224)
target_tile = 512
source_tile = 512


def thirds(values):
    high = values.astype(bf16)
    rest = values - high.astype(f32)
    middle = rest.astype(bf16)
    low = (rest - middle.astype(f32)).astype(bf16)
    return high, middle, low


def pick_rows(rows, shape):
    at = lax.broadcasted_iota(jnp.int32, shape, 0)
    out = jnp.zeros(shape, f32)
    for k, row in enumerate(rows):
        out = jnp.where(at == k, jnp.broadcast_to(row, shape), out)
    return out


def put_thirds(ref, values, outer):
    parts = [part.astype(f32) for part in thirds(values)]
    for p in range(3):
        for q in range(3):
            k = 3 * p + q
            ref[8 * k : 8 * k + 8, :] = parts[p if outer else q]


def sketch_kernel(targets, sources, weights, usable, omega, tiles, sketch,
                  feature, tfeat, afeat, bfeat, masked, a_even, b_even, k_even, a_odd, b_odd, k_odd, acc):
    step = pl.program_id(0)
    nrows, ncols = targets.shape[1], sources.shape[1]
    per_step = nrows // target_tile
    total = per_step * (ncols // source_tile)

    def block(at, size):
        return pl.ds(pl.multiple_of(at * size, size), size)

    def distances(tile, a_buf, b_buf):
        here = tfeat[block(lax.rem(tile, per_step), target_tile), :]
        there = block(lax.div(tile, per_step), source_tile)
        a_buf[...] = jnp.dot(here, afeat[:, there], preferred_element_type=f32)
        b_buf[...] = jnp.dot(here, bfeat[:, there], preferred_element_type=f32)

    def evaluate(tile, a_buf, b_buf, k_buf):
        first = lax.rem(tile, per_step) * target_tile
        for r in range(0, target_tile, 16):
            over = lax.rsqrt(a_buf[r : r + 16, :])
            turn = b_buf[r : r + 16, :] * over
            away = 0.25 - jnp.abs(turn - jnp.round(turn))
            square = away * away
            c0, c1, c2, c3 = (turns * c for c in sine)
            wave = ((c3 * square + c2) * square + c1) * square + c0
            low = ((wave * away) * over).astype(bf16)
            k_buf[r : r + 16, :] = low
            tiles[pl.ds(pl.multiple_of(first + r, 16), 16), :] = low

    def accumulate(tile, k_buf):
        rows = block(lax.rem(tile, per_step), target_tile)
        there = block(lax.div(tile, per_step), source_tile)
        acc[rows, :] += jnp.dot(k_buf[...], masked[there, :], preferred_element_type=f32)

    @pl.when(step == 0)
    def _():
        feature[...] = jnp.zeros_like(feature)
        tx = (targets[0:1, :] - (0.5 + 0.5 * separation)) * turns
        ty = (targets[1:2, :] - 0.5) * turns
        tz = (targets[2:3, :] - 0.5) * turns
        rows = [tx, ty, tz, tx * tx + ty * ty + tz * tz, jnp.ones_like(tx)]
        view = feature.at[:, 0:nrows]
        put_thirds(view, pick_rows(rows, (8, nrows)), True)
        for k in range(nrows // 128):
            tfeat[128 * k : 128 * k + 128, :] = feature[:, 128 * k : 128 * k + 128].T.astype(bf16)
        sx = (sources[0:1, :] + (0.5 * separation - 0.5)) * turns
        sy = (sources[1:2, :] - 0.5) * turns
        sz = (sources[2:3, :] - 0.5) * turns
        norm = sx * sx + sy * sy + sz * sz
        inverse = 1.0 / weights[...]
        for ref, scale in ((bfeat, inverse), (afeat, inverse * inverse)):
            rows = [-2.0 * sx * scale, -2.0 * sy * scale, -2.0 * sz * scale, scale, norm * scale]
            put_thirds(feature, pick_rows(rows, (8, ncols)), False)
            ref[...] = feature[...].astype(bf16)
        flag = pick_rows([usable[...]], (8, ncols)).astype(bf16)
        column = lax.dot_general(
            flag, jnp.ones((8, omega.shape[1]), bf16), (((0,), (0,)), ((), ())), preferred_element_type=f32
        )
        masked[...] = (omega[...].astype(f32) * column).astype(bf16)
        acc[...] = jnp.zeros_like(acc)
        k_odd[...] = jnp.zeros_like(k_odd)
        distances(0, a_even, b_even)

    def pair(p, carry):
        tile = step * per_step + 2 * p
        distances(tile + 1, a_odd, b_odd)
        evaluate(tile, a_even, b_even, k_even)
        accumulate(jnp.maximum(tile - 1, 0), k_odd)
        distances(jnp.minimum(tile + 2, total - 1), a_even, b_even)
        evaluate(tile + 1, a_odd, b_odd, k_odd)
        accumulate(tile, k_even)
        return carry

    lax.fori_loop(0, per_step // 2, pair, 0)

    @pl.when(step == pl.num_programs(0) - 1)
    def _():
        accumulate(total - 1, k_odd)
        sketch[...] = acc[...].astype(bf16)


def make_sketch(targets, sources, weights, usable, omega):
    nrows, ncols, rank = targets.shape[1], sources.shape[1], omega.shape[1]
    whole = lambda i: (0, 0)
    once = dict(pipeline_mode=pl.Buffered(1))
    return pl.pallas_call(
        sketch_kernel,
        grid=(ncols // source_tile,),
        in_specs=[
            pl.BlockSpec((3, nrows), whole, **once),
            pl.BlockSpec((3, ncols), whole, **once),
            pl.BlockSpec((1, ncols), whole, **once),
            pl.BlockSpec((1, ncols), whole, **once),
            pl.BlockSpec((ncols, rank), whole, **once),
        ],
        out_specs=[
            pl.BlockSpec((nrows, source_tile), lambda j: (0, j)),
            pl.BlockSpec((nrows, rank), whole),
        ],
        out_shape=[
            jax.ShapeDtypeStruct((nrows, ncols), bf16),
            jax.ShapeDtypeStruct((nrows, rank), bf16),
        ],
        scratch_shapes=[
            pltpu.VMEM((128, ncols), f32),
            pltpu.VMEM((nrows, 128), bf16),
            pltpu.VMEM((128, ncols), bf16),
            pltpu.VMEM((128, ncols), bf16),
            pltpu.VMEM((ncols, rank), bf16),
            pltpu.VMEM((target_tile, source_tile), f32),
            pltpu.VMEM((target_tile, source_tile), f32),
            pltpu.VMEM((target_tile, source_tile), bf16),
            pltpu.VMEM((target_tile, source_tile), f32),
            pltpu.VMEM((target_tile, source_tile), f32),
            pltpu.VMEM((target_tile, source_tile), bf16),
            pltpu.VMEM((nrows, rank), f32),
        ],
        name="sketch",
    )(targets, sources, weights, usable, omega)


def piece_kernel(parts, out):
    total = parts[0].astype(f32)
    for k in range(1, parts.shape[0]):
        total += parts[k].astype(f32)
    for k in range(out.shape[0]):
        out[k] = total


def add_pieces(parts):
    return pl.pallas_call(
        piece_kernel, out_shape=jax.ShapeDtypeStruct(parts.shape, f32), name="pieces"
    )(parts)


def project_kernel(sketch, tiles, usable, out, flipped, gram):
    rank = sketch.shape[1]
    band = gram.shape[0] // lax.axis_size("cols")

    @pl.when(pl.program_id(0) == 0)
    def _():
        whole = sketch[...]
        upper = whole.astype(bf16)
        lower = (whole - upper.astype(f32)).astype(bf16)
        contract = (((0,), (0,)), ((), ()))
        flipped[...] = upper.astype(f32).T.astype(bf16)
        cross = lax.dot_general(upper, lower, contract, preferred_element_type=f32)
        gram[...] = lax.dot_general(lower, lower, contract, preferred_element_type=f32) + (cross + cross.T)
        gram[...] += jnp.dot(flipped[...], upper, preferred_element_type=f32)

    product = jnp.dot(flipped[...], tiles[...], preferred_element_type=f32)
    product = (product * usable[...]).astype(bf16)
    first = pl.multiple_of(lax.axis_index("cols") * band, band)
    own = jnp.concatenate([part.astype(f32) for part in thirds(gram[pl.ds(first, band), :])], axis=0)
    own = own.astype(bf16)
    for k in range(out.shape[0]):
        out[k, 0:rank, :] = product[:, 128 * k : 128 * k + 128]
        out[k, rank:, :] = own


def project(sketch, tiles, usable, row_devices):
    nrows, ncols = tiles.shape
    rank = sketch.shape[1]
    width = 512
    dests = width // (ncols // row_devices)
    return pl.pallas_call(
        project_kernel,
        grid=(ncols // width,),
        in_specs=[
            pl.BlockSpec((nrows, rank), lambda j: (0, 0), pipeline_mode=pl.Buffered(1)),
            pl.BlockSpec((nrows, width), lambda j: (0, j)),
            pl.BlockSpec((1, width), lambda j: (0, j)),
        ],
        out_specs=pl.BlockSpec((dests, rank + 24, 128), lambda j: (j, 0, 0)),
        out_shape=jax.ShapeDtypeStruct((row_devices, rank + 24, 128), bf16),
        scratch_shapes=[pltpu.VMEM((rank, nrows), bf16), pltpu.VMEM((rank, rank), f32)],
        name="project",
    )(sketch, tiles, usable)


def fold_kernel(parts, product, band):
    total = parts[0].astype(f32)
    for k in range(1, parts.shape[0]):
        total += parts[k].astype(f32)
    rank = product.shape[0]
    rows = band.shape[1]
    product[...] = total[0:rank]
    own = total[rank : rank + rows] + (
        total[rank + rows : rank + 2 * rows] + total[rank + 2 * rows : rank + 3 * rows]
    )
    for k in range(band.shape[0]):
        band[k] = own


def fold(parts, col_devices):
    rank = parts.shape[1] - 24
    return pl.pallas_call(
        fold_kernel,
        out_shape=[
            jax.ShapeDtypeStruct((rank, rank), f32),
            jax.ShapeDtypeStruct((col_devices, rank // col_devices, rank), f32),
        ],
        name="fold",
    )(parts)


def inverse_factor(bands):
    count, _, rank = bands.shape
    at_row = lax.broadcasted_iota(jnp.int32, (8, rank), 0)
    at_col = lax.broadcasted_iota(jnp.int32, (8, rank), 1)
    left = [bands[i] for i in range(count)]
    right = [jnp.where(at_col == at_row + 8 * i, 1.0, 0.0) for i in range(count)]
    for k in range(rank):
        block, r = divmod(k, 8)
        row = jnp.broadcast_to(left[block][r : r + 1, :], (8, rank))
        other = jnp.broadcast_to(right[block][r : r + 1, :], (8, rank))
        pivot = 1.0 / jnp.broadcast_to(row[:, k : k + 1], (8, rank))
        for i in range(block, count):
            if i == block and r == 7:
                continue
            factor = jnp.broadcast_to(left[i][:, k : k + 1], (8, rank)) * pivot
            if i == block:
                factor = jnp.where(at_row > r, factor, 0.0)
            left[i] = left[i] - factor * row
            right[i] = right[i] - factor * other
    out = []
    for i in range(count):
        diagonal = jnp.sum(jnp.where(at_col == at_row + 8 * i, left[i], 0.0), axis=1, keepdims=True)
        out.append(right[i] * lax.rsqrt(jnp.broadcast_to(diagonal, (8, rank))))
    return out


def finish_kernel(scale, sketch, product, bands, basis, projected, inverse):
    for i, rows in enumerate(inverse_factor(bands)):
        inverse[8 * i : 8 * i + 8, :] = rows
    contract = (((1,), (1,)), ((), ()))
    high, middle, low = thirds(inverse[...] * scale)
    whole = sketch[...]
    upper = whole.astype(bf16)
    lower = (whole - upper.astype(f32)).astype(bf16)
    total = lax.dot_general(upper, low, contract, preferred_element_type=f32)
    total += lax.dot_general(lower, middle, contract, preferred_element_type=f32)
    total += lax.dot_general(lower, high, contract, preferred_element_type=f32)
    total += lax.dot_general(upper, middle, contract, preferred_element_type=f32)
    basis[...] = total + lax.dot_general(upper, high, contract, preferred_element_type=f32)
    projected[...] = lax.dot_general(
        product[...].T,
        inverse[...],
        contract,
        precision=lax.Precision.HIGHEST,
        preferred_element_type=f32,
    )


def finish(sketch, product, bands, scale):
    return pl.pallas_call(
        functools.partial(finish_kernel, scale),
        out_shape=[
            jax.ShapeDtypeStruct(sketch.shape, f32),
            jax.ShapeDtypeStruct(product.shape, f32),
        ],
        scratch_shapes=[pltpu.VMEM(product.shape, f32)],
        name="finish",
    )(sketch, product, bands)


def shards(targets, sources, weights, counts, omega):
    rows_here, cols_here, rank = targets.shape[1], sources.shape[1], omega.shape[1]
    row_devices, col_devices = lax.axis_size("rows"), lax.axis_size("cols")
    panel_count = counts.shape[0]
    usable = (
        (lax.broadcasted_iota(jnp.int32, (panel_count, cols_here // panel_count), 1) < counts[:, None])
        .reshape(1, cols_here)
        .astype(f32)
    )
    tiles, partial = make_sketch(targets, sources, weights.reshape(1, cols_here), usable, omega)
    pieces = lax.all_to_all(partial.reshape(col_devices, -1, rank), "cols", 0, 0)
    sketch = lax.all_to_all(add_pieces(pieces), "cols", 0, 0).reshape(rows_here, rank)
    terms = lax.all_to_all(project(sketch, tiles, usable, row_devices), "rows", 0, 0)
    product, band = fold(terms, col_devices)
    bands = lax.all_to_all(band, "cols", 0, 0)
    return finish(sketch, product, bands, math.sqrt(rows_here * row_devices))


def solution(mesh):
    return jax.shard_map(
        shards,
        mesh=mesh,
        in_specs=(P(None, "rows"), P(None, "cols"), P("cols"), P("cols"), P("cols", None)),
        out_specs=(P("rows", None), P(("cols", "rows"), None)),
        check_vma=False,
    )
```

```python
import functools
import math

import jax
import jax.numpy as jnp
from jax import lax
from jax.experimental import pallas as pl
from jax.experimental.pallas import tpu as pltpu
from jax.sharding import PartitionSpec as P

f32 = jnp.float32
bf16 = jnp.bfloat16
wave_number = 160.0
separation = 2.0
turns = wave_number / (2.0 * math.pi)
sine = (6.283164043875678, -41.33714231633244, 81.34076713243772, -70.99341720807224)
target_tile = 512
source_tile = 512


def thirds(values):
    high = values.astype(bf16)
    rest = values - high.astype(f32)
    middle = rest.astype(bf16)
    low = (rest - middle.astype(f32)).astype(bf16)
    return high, middle, low


def pick_rows(rows, shape):
    at = lax.broadcasted_iota(jnp.int32, shape, 0)
    out = jnp.zeros(shape, f32)
    for k, row in enumerate(rows):
        out = jnp.where(at == k, jnp.broadcast_to(row, shape), out)
    return out


def put_thirds(ref, values, outer):
    parts = [part.astype(f32) for part in thirds(values)]
    for p in range(3):
        for q in range(3):
            k = 3 * p + q
            ref[8 * k : 8 * k + 8, :] = parts[p if outer else q]


def sketch_kernel(targets, sources, weights, usable, omega, tiles, sketch,
                  feature, tfeat, afeat, bfeat, masked, a_even, b_even, k_even, a_odd, b_odd, k_odd, acc):
    step = pl.program_id(0)
    nrows, ncols = targets.shape[1], sources.shape[1]
    per_step = nrows // target_tile
    total = per_step * (ncols // source_tile)

    def block(at, size):
        return pl.ds(pl.multiple_of(at * size, size), size)

    def distances(tile, a_buf, b_buf):
        here = tfeat[block(lax.rem(tile, per_step), target_tile), :]
        there = block(lax.div(tile, per_step), source_tile)
        a_buf[...] = jnp.dot(here, afeat[:, there], preferred_element_type=f32)
        b_buf[...] = jnp.dot(here, bfeat[:, there], preferred_element_type=f32)

    def evaluate(tile, a_buf, b_buf, k_buf):
        first = lax.rem(tile, per_step) * target_tile
        for r in range(0, target_tile, 16):
            over = lax.rsqrt(a_buf[r : r + 16, :])
            turn = b_buf[r : r + 16, :] * over
            away = 0.25 - jnp.abs(turn - jnp.round(turn))
            square = away * away
            c0, c1, c2, c3 = (turns * c for c in sine)
            wave = ((c3 * square + c2) * square + c1) * square + c0
            low = ((wave * away) * over).astype(bf16)
            k_buf[r : r + 16, :] = low
            tiles[pl.ds(pl.multiple_of(first + r, 16), 16), :] = low

    def accumulate(tile, k_buf):
        rows = block(lax.rem(tile, per_step), target_tile)
        there = block(lax.div(tile, per_step), source_tile)
        acc[rows, :] += jnp.dot(k_buf[...], masked[there, :], preferred_element_type=f32)

    @pl.when(step == 0)
    def _():
        feature[...] = jnp.zeros_like(feature)
        tx = (targets[0:1, :] - (0.5 + 0.5 * separation)) * turns
        ty = (targets[1:2, :] - 0.5) * turns
        tz = (targets[2:3, :] - 0.5) * turns
        rows = [tx, ty, tz, tx * tx + ty * ty + tz * tz, jnp.ones_like(tx)]
        view = feature.at[:, 0:nrows]
        put_thirds(view, pick_rows(rows, (8, nrows)), True)
        for k in range(nrows // 128):
            tfeat[128 * k : 128 * k + 128, :] = feature[:, 128 * k : 128 * k + 128].T.astype(bf16)
        sx = (sources[0:1, :] + (0.5 * separation - 0.5)) * turns
        sy = (sources[1:2, :] - 0.5) * turns
        sz = (sources[2:3, :] - 0.5) * turns
        norm = sx * sx + sy * sy + sz * sz
        inverse = 1.0 / weights[...]
        for ref, scale in ((bfeat, inverse), (afeat, inverse * inverse)):
            rows = [-2.0 * sx * scale, -2.0 * sy * scale, -2.0 * sz * scale, scale, norm * scale]
            put_thirds(feature, pick_rows(rows, (8, ncols)), False)
            ref[...] = feature[...].astype(bf16)
        flag = pick_rows([usable[...]], (8, ncols)).astype(bf16)
        column = lax.dot_general(
            flag, jnp.ones((8, omega.shape[1]), bf16), (((0,), (0,)), ((), ())), preferred_element_type=f32
        )
        masked[...] = (omega[...].astype(f32) * column).astype(bf16)
        acc[...] = jnp.zeros_like(acc)
        k_odd[...] = jnp.zeros_like(k_odd)
        distances(0, a_even, b_even)

    def pair(p, carry):
        tile = step * per_step + 2 * p
        distances(tile + 1, a_odd, b_odd)
        evaluate(tile, a_even, b_even, k_even)
        accumulate(jnp.maximum(tile - 1, 0), k_odd)
        distances(jnp.minimum(tile + 2, total - 1), a_even, b_even)
        evaluate(tile + 1, a_odd, b_odd, k_odd)
        accumulate(tile, k_even)
        return carry

    lax.fori_loop(0, per_step // 2, pair, 0)

    @pl.when(step == pl.num_programs(0) - 1)
    def _():
        accumulate(total - 1, k_odd)
        sketch[...] = acc[...].astype(bf16)


def make_sketch(targets, sources, weights, usable, omega):
    nrows, ncols, rank = targets.shape[1], sources.shape[1], omega.shape[1]
    whole = lambda i: (0, 0)
    once = dict(pipeline_mode=pl.Buffered(1))
    return pl.pallas_call(
        sketch_kernel,
        grid=(ncols // source_tile,),
        in_specs=[
            pl.BlockSpec((3, nrows), whole, **once),
            pl.BlockSpec((3, ncols), whole, **once),
            pl.BlockSpec((1, ncols), whole, **once),
            pl.BlockSpec((1, ncols), whole, **once),
            pl.BlockSpec((ncols, rank), whole, **once),
        ],
        out_specs=[
            pl.BlockSpec((nrows, source_tile), lambda j: (0, j)),
            pl.BlockSpec((nrows, rank), whole),
        ],
        out_shape=[
            jax.ShapeDtypeStruct((nrows, ncols), bf16),
            jax.ShapeDtypeStruct((nrows, rank), bf16),
        ],
        scratch_shapes=[
            pltpu.VMEM((128, ncols), f32),
            pltpu.VMEM((nrows, 128), bf16),
            pltpu.VMEM((128, ncols), bf16),
            pltpu.VMEM((128, ncols), bf16),
            pltpu.VMEM((ncols, rank), bf16),
            pltpu.VMEM((target_tile, source_tile), f32),
            pltpu.VMEM((target_tile, source_tile), f32),
            pltpu.VMEM((target_tile, source_tile), bf16),
            pltpu.VMEM((target_tile, source_tile), f32),
            pltpu.VMEM((target_tile, source_tile), f32),
            pltpu.VMEM((target_tile, source_tile), bf16),
            pltpu.VMEM((nrows, rank), f32),
        ],
        name="sketch", compiler_params=pltpu.CompilerParams(vmem_limit_bytes=24 << 20),
    )(targets, sources, weights, usable, omega)


def piece_kernel(parts, out):
    total = parts[0].astype(f32)
    for k in range(1, parts.shape[0]):
        total += parts[k].astype(f32)
    for k in range(out.shape[0]):
        out[k] = total


def add_pieces(parts):
    return pl.pallas_call(
        piece_kernel, out_shape=jax.ShapeDtypeStruct(parts.shape, f32), name="pieces", compiler_params=pltpu.CompilerParams(vmem_limit_bytes=6 << 20)
    )(parts)


def project_kernel(sketch, tiles, usable, out, flipped, gram):
    rank = sketch.shape[1]
    band = gram.shape[0] // lax.axis_size("cols")

    @pl.when(pl.program_id(0) == 0)
    def _():
        whole = sketch[...]
        upper = whole.astype(bf16)
        lower = (whole - upper.astype(f32)).astype(bf16)
        contract = (((0,), (0,)), ((), ()))
        flipped[...] = upper.astype(f32).T.astype(bf16)
        cross = lax.dot_general(upper, lower, contract, preferred_element_type=f32)
        gram[...] = lax.dot_general(lower, lower, contract, preferred_element_type=f32) + (cross + cross.T)
        gram[...] += jnp.dot(flipped[...], upper, preferred_element_type=f32)

    product = jnp.dot(flipped[...], tiles[...], preferred_element_type=f32)
    product = (product * usable[...]).astype(bf16)
    first = pl.multiple_of(lax.axis_index("cols") * band, band)
    own = jnp.concatenate([part.astype(f32) for part in thirds(gram[pl.ds(first, band), :])], axis=0)
    own = own.astype(bf16)
    for k in range(out.shape[0]):
        out[k, 0:rank, :] = product[:, 128 * k : 128 * k + 128]
        out[k, rank:, :] = own


def project(sketch, tiles, usable, row_devices):
    nrows, ncols = tiles.shape
    rank = sketch.shape[1]
    width = 512
    dests = width // (ncols // row_devices)
    return pl.pallas_call(
        project_kernel,
        grid=(ncols // width,),
        in_specs=[
            pl.BlockSpec((nrows, rank), lambda j: (0, 0), pipeline_mode=pl.Buffered(1)),
            pl.BlockSpec((nrows, width), lambda j: (0, j)),
            pl.BlockSpec((1, width), lambda j: (0, j)),
        ],
        out_specs=pl.BlockSpec((dests, rank + 24, 128), lambda j: (j, 0, 0)),
        out_shape=jax.ShapeDtypeStruct((row_devices, rank + 24, 128), bf16),
        scratch_shapes=[pltpu.VMEM((rank, nrows), bf16), pltpu.VMEM((rank, rank), f32)],
        name="project", compiler_params=pltpu.CompilerParams(vmem_limit_bytes=14 << 20),
    )(sketch, tiles, usable)


def fold_kernel(parts, product, band):
    total = parts[0].astype(f32)
    for k in range(1, parts.shape[0]):
        total += parts[k].astype(f32)
    rank = product.shape[0]
    rows = band.shape[1]
    product[...] = total[0:rank]
    own = total[rank : rank + rows] + (
        total[rank + rows : rank + 2 * rows] + total[rank + 2 * rows : rank + 3 * rows]
    )
    for k in range(band.shape[0]):
        band[k] = own


def fold(parts, col_devices):
    rank = parts.shape[1] - 24
    return pl.pallas_call(
        fold_kernel,
        out_shape=[
            jax.ShapeDtypeStruct((rank, rank), f32),
            jax.ShapeDtypeStruct((col_devices, rank // col_devices, rank), f32),
        ],
        name="fold", compiler_params=pltpu.CompilerParams(vmem_limit_bytes=6 << 20),
    )(parts)


def inverse_factor(bands):
    count, _, rank = bands.shape
    shape = (8, rank)
    at_row = lax.broadcasted_iota(jnp.int32, shape, 0)
    at_col = lax.broadcasted_iota(jnp.int32, shape, 1)
    left = [bands[i] for i in range(count)]
    right = [jnp.where(at_col == at_row + 8 * i, 1.0, 0.0) for i in range(count)]
    inside = at_row < 8

    def along_lanes(values, k):
        return jnp.where(inside, jnp.broadcast_to(values[:, k : k + 1], shape), 0.0)

    def along_rows(values, r):
        return jnp.broadcast_to(values[r : r + 1, :], shape)

    for k in range(0, rank, 2):
        block, r = divmod(k, 8)
        first = [along_lanes(left[i], k) for i in range(block, count)]
        second = [along_lanes(left[i], k + 1) for i in range(block, count)]
        a, b, c = along_rows(first[0], r), along_rows(first[0], r + 1), along_rows(second[0], r + 1)
        scale = 1.0 / (a * c - b * b)
        a_s, b_s, c_s = a * scale, b * scale, c * scale
        upper, lower = along_rows(left[block], r), along_rows(left[block], r + 1)
        upper_r, lower_r = along_rows(right[block], r), along_rows(right[block], r + 1)
        for i in range(block, count):
            if i == block and r == 6:
                continue
            one, two = first[i - block], second[i - block]
            u = one * c_s - two * b_s
            v = two * a_s - one * b_s
            if i == block:
                u = jnp.where(at_row > r + 1, u, 0.0)
                v = jnp.where(at_row > r + 1, v, 0.0)
            left[i] = left[i] - (u * upper + v * lower)
            right[i] = right[i] - (u * upper_r + v * lower_r)
        ratio = jnp.where(at_row == r + 1, b * (1.0 / a), 0.0)
        left[block] = left[block] - ratio * upper
        right[block] = right[block] - ratio * upper_r
    out = []
    for i in range(count):
        diagonal = jnp.sum(jnp.where(at_col == at_row + 8 * i, left[i], 0.0), axis=1, keepdims=True)
        out.append(right[i] * lax.rsqrt(jnp.broadcast_to(diagonal, shape)))
    return out


def finish_kernel(scale, sketch, product, bands, basis, projected, inverse):
    for i, rows in enumerate(inverse_factor(bands)):
        inverse[8 * i : 8 * i + 8, :] = rows
    contract = (((1,), (1,)), ((), ()))
    high, middle, low = thirds(inverse[...] * scale)
    whole = sketch[...]
    upper = whole.astype(bf16)
    lower = (whole - upper.astype(f32)).astype(bf16)
    total = lax.dot_general(upper, low, contract, preferred_element_type=f32)
    total += lax.dot_general(lower, middle, contract, preferred_element_type=f32)
    total += lax.dot_general(lower, high, contract, preferred_element_type=f32)
    total += lax.dot_general(upper, middle, contract, preferred_element_type=f32)
    basis[...] = total + lax.dot_general(upper, high, contract, preferred_element_type=f32)
    projected[...] = lax.dot_general(
        product[...].T,
        inverse[...],
        contract,
        precision=lax.Precision.HIGHEST,
        preferred_element_type=f32,
    )


def finish(sketch, product, bands, scale):
    return pl.pallas_call(
        functools.partial(finish_kernel, scale),
        out_shape=[
            jax.ShapeDtypeStruct(sketch.shape, f32),
            jax.ShapeDtypeStruct(product.shape, f32),
        ],
        scratch_shapes=[pltpu.VMEM(product.shape, f32)],
        name="finish", compiler_params=pltpu.CompilerParams(vmem_limit_bytes=8 << 20),
    )(sketch, product, bands)


def shards(targets, sources, weights, counts, omega):
    rows_here, cols_here, rank = targets.shape[1], sources.shape[1], omega.shape[1]
    row_devices, col_devices = lax.axis_size("rows"), lax.axis_size("cols")
    panel_count = counts.shape[0]
    usable = (
        (lax.broadcasted_iota(jnp.int32, (panel_count, cols_here // panel_count), 1) < counts[:, None])
        .reshape(1, cols_here)
        .astype(f32)
    )
    tiles, partial = make_sketch(targets, sources, weights.reshape(1, cols_here), usable, omega)
    pieces = lax.all_to_all(partial.reshape(col_devices, -1, rank), "cols", 0, 0)
    sketch = lax.all_to_all(add_pieces(pieces), "cols", 0, 0).reshape(rows_here, rank)
    terms = lax.all_to_all(project(sketch, tiles, usable, row_devices), "rows", 0, 0)
    product, band = fold(terms, col_devices)
    bands = lax.all_to_all(band, "cols", 0, 0)
    return finish(sketch, product, bands, math.sqrt(rows_here * row_devices))


def solution(mesh):
    return jax.shard_map(
        shards,
        mesh=mesh,
        in_specs=(P(None, "rows"), P(None, "cols"), P("cols"), P("cols"), P("cols", None)),
        out_specs=(P("rows", None), P(("cols", "rows"), None)),
        check_vma=False,
    )
```

```python
import functools
import math

import jax
import jax.numpy as jnp
from jax import lax
from jax.experimental import pallas as pl
from jax.experimental.pallas import tpu as pltpu
from jax.sharding import PartitionSpec as P

f32 = jnp.float32
bf16 = jnp.bfloat16
wave_number = 160.0
separation = 2.0
turns = wave_number / (2.0 * math.pi)
sine = (6.283164043875678, -41.33714231633244, 81.34076713243772, -70.99341720807224)
target_tile = 512
source_tile = 512


def thirds(values):
    high = values.astype(bf16)
    rest = values - high.astype(f32)
    middle = rest.astype(bf16)
    low = (rest - middle.astype(f32)).astype(bf16)
    return high, middle, low


def pick_rows(rows, shape):
    at = lax.broadcasted_iota(jnp.int32, shape, 0)
    out = jnp.zeros(shape, f32)
    for k, row in enumerate(rows):
        out = jnp.where(at == k, jnp.broadcast_to(row, shape), out)
    return out


def put_thirds(ref, values, outer):
    parts = [part.astype(f32) for part in thirds(values)]
    for p in range(3):
        for q in range(3):
            k = 3 * p + q
            ref[8 * k : 8 * k + 8, :] = parts[p if outer else q]


def halves():
    own = lax.rem(lax.axis_index("cols"), 2)
    return own, 1 - own


def sketch_kernel(targets_in, sources_in, weights_in, counts_in, omega_in, tiles, sketch, usable,
                  targets, sources, weights, counts, omega, arrived, feature, tfeat, afeat, bfeat, masked, a_even, b_even, k_even, a_odd, b_odd, k_odd, acc):
    step = pl.program_id(0)
    nrows, ncols = targets.shape[1], sources.shape[1]
    per_step = nrows // target_tile
    total = per_step * (ncols // source_tile)

    def block(at, size):
        return pl.ds(pl.multiple_of(at * size, size), size)

    def distances(tile, a_buf, b_buf):
        here = tfeat[block(lax.rem(tile, per_step), target_tile), :]
        there = block(lax.div(tile, per_step), source_tile)
        a_buf[...] = jnp.dot(here, afeat[:, there], preferred_element_type=f32)
        b_buf[...] = jnp.dot(here, bfeat[:, there], preferred_element_type=f32)

    def evaluate(tile, a_buf, b_buf, k_buf):
        first = lax.rem(tile, per_step) * target_tile
        for r in range(0, target_tile, 16):
            over = lax.rsqrt(a_buf[r : r + 16, :])
            turn = b_buf[r : r + 16, :] * over
            away = 0.25 - jnp.abs(turn - jnp.round(turn))
            square = away * away
            c0, c1, c2, c3 = (turns * c for c in sine)
            wave = ((c3 * square + c2) * square + c1) * square + c0
            low = ((wave * away) * over).astype(bf16)
            k_buf[r : r + 16, :] = low
            tiles[pl.ds(pl.multiple_of(first + r, 16), 16), :] = low

    def accumulate(tile, k_buf):
        rows = block(lax.rem(tile, per_step), target_tile)
        there = block(lax.div(tile, per_step), source_tile)
        acc[rows, :] += jnp.dot(k_buf[...], masked[there, :], preferred_element_type=f32)

    own, other = halves()
    half = nrows // 2
    pieces, rank = sketch.shape[0], sketch.shape[2]
    share = half // pieces

    @pl.when(step == 0)
    def _():
        moves = [
            pltpu.make_async_copy(source, target, arrived.at[k])
            for k, (source, target) in enumerate(
                [(targets_in, targets), (sources_in, sources), (weights_in, weights), (counts_in, counts), (omega_in, omega)]
            )
        ]
        for move in moves:
            move.start()
        feature[...] = jnp.zeros_like(feature)
        moves[0].wait()
        tx = (targets[0:1, :] - (0.5 + 0.5 * separation)) * turns
        ty = (targets[1:2, :] - 0.5) * turns
        tz = (targets[2:3, :] - 0.5) * turns
        rows = [tx, ty, tz, tx * tx + ty * ty + tz * tz, jnp.ones_like(tx)]
        view = feature.at[:, 0:nrows]
        put_thirds(view, pick_rows(rows, (8, nrows)), True)
        for k in range(pieces):
            block_rows = feature[:, 2 * share * k : 2 * share * (k + 1)].T.astype(bf16)
            tfeat[pl.ds(pl.multiple_of(own * half + share * k, share), share), :] = block_rows[0:share]
            tfeat[pl.ds(pl.multiple_of(other * half + share * k, share), share), :] = block_rows[share : 2 * share]
        for move in moves[1:4]:
            move.wait()
        sx = (sources[0:1, :] + (0.5 * separation - 0.5)) * turns
        sy = (sources[1:2, :] - 0.5) * turns
        sz = (sources[2:3, :] - 0.5) * turns
        norm = sx * sx + sy * sy + sz * sz
        inverse = 1.0 / weights[...]
        for ref, scale in ((bfeat, inverse), (afeat, inverse * inverse)):
            rows = [-2.0 * sx * scale, -2.0 * sy * scale, -2.0 * sz * scale, scale, norm * scale]
            put_thirds(feature, pick_rows(rows, (8, ncols)), False)
            ref[...] = feature[...].astype(bf16)
        panels = counts.shape[1]
        size = ncols // panels
        span = 128 // size
        shape = (ncols // 128, panels)
        mine = lax.shift_right_logical(lax.broadcasted_iota(jnp.int32, shape, 1), span.bit_length() - 1) == lax.broadcasted_iota(jnp.int32, shape, 0)
        chosen = jnp.where(mine, jnp.broadcast_to(counts[...].astype(f32), shape), 0.0).astype(bf16)
        shape = (panels, 128)
        spread = (lax.broadcasted_iota(jnp.int32, shape, 0) & (span - 1)) == lax.shift_right_logical(lax.broadcasted_iota(jnp.int32, shape, 1), size.bit_length() - 1)
        filled = jnp.dot(chosen, jnp.where(spread, 1.0, 0.0).astype(bf16), preferred_element_type=f32)
        lane = (lax.broadcasted_iota(jnp.int32, filled.shape, 1) & (size - 1)).astype(f32)
        flags = jnp.where(lane < filled, 1.0, 0.0)
        for k in range(ncols // 128):
            usable[0:1, 128 * k : 128 * k + 128] = flags[k : k + 1, :]
        moves[4].wait()
        distances(0, a_even, b_even)
        columns = flags.T
        for k in range(ncols // 128):
            rows = slice(128 * k, 128 * k + 128)
            flag = jnp.broadcast_to(columns[:, k : k + 1], (128, rank))
            masked[rows, :] = (omega[rows, :].astype(f32) * flag).astype(bf16)
        acc[...] = jnp.zeros_like(acc)
        k_odd[...] = jnp.zeros_like(k_odd)

    def pair(p, carry):
        tile = step * per_step + 2 * p
        distances(tile + 1, a_odd, b_odd)
        evaluate(tile, a_even, b_even, k_even)
        accumulate(jnp.maximum(tile - 1, 0), k_odd)
        distances(jnp.minimum(tile + 2, total - 1), a_even, b_even)
        evaluate(tile + 1, a_odd, b_odd, k_odd)
        accumulate(tile, k_even)
        return carry

    lax.fori_loop(0, per_step // 2, pair, 0)

    @pl.when(step == pl.num_programs(0) - 1)
    def _():
        accumulate(total - 1, k_odd)
        for k in range(pieces):
            for part, keeper in ((0, own), (1, other)):
                rows = pl.ds(pl.multiple_of(keeper * half + share * k, share), share)
                sketch[k, part * share : (part + 1) * share, :] = acc[rows, :].astype(bf16)


def make_sketch(targets, sources, weights, counts, omega, col_devices):
    nrows, ncols, rank = targets.shape[1], sources.shape[1], omega.shape[1]
    operands = [pltpu.with_memory_space_constraint(x, pltpu.HBM) for x in (targets, sources, weights, counts, omega)]
    return pl.pallas_call(
        sketch_kernel,
        grid=(ncols // source_tile,),
        in_specs=[pl.BlockSpec(memory_space=pltpu.HBM)] * 5,
        out_specs=[
            pl.BlockSpec((nrows, source_tile), lambda j: (0, j)),
            pl.BlockSpec((col_devices, nrows // col_devices, rank), lambda j: (0, 0, 0)),
            pl.BlockSpec((1, ncols), lambda j: (0, 0)),
        ],
        out_shape=[
            jax.ShapeDtypeStruct((nrows, ncols), bf16),
            jax.ShapeDtypeStruct((col_devices, nrows // col_devices, rank), bf16),
            jax.ShapeDtypeStruct((1, ncols), f32),
        ],
        scratch_shapes=[
            pltpu.VMEM((3, nrows), f32),
            pltpu.VMEM((3, ncols), f32),
            pltpu.VMEM((1, ncols), f32),
            pltpu.VMEM(counts.shape, jnp.int32),
            pltpu.VMEM((ncols, rank), bf16),
            pltpu.SemaphoreType.DMA((5,)),
            pltpu.VMEM((128, ncols), f32),
            pltpu.VMEM((nrows, 128), bf16),
            pltpu.VMEM((128, ncols), bf16),
            pltpu.VMEM((128, ncols), bf16),
            pltpu.VMEM((ncols, rank), bf16),
            pltpu.VMEM((target_tile, source_tile), f32),
            pltpu.VMEM((target_tile, source_tile), f32),
            pltpu.VMEM((target_tile, source_tile), bf16),
            pltpu.VMEM((target_tile, source_tile), f32),
            pltpu.VMEM((target_tile, source_tile), f32),
            pltpu.VMEM((target_tile, source_tile), bf16),
            pltpu.VMEM((nrows, rank), f32),
        ],
        name="sketch", compiler_params=pltpu.CompilerParams(vmem_limit_bytes=24 << 20),
    )(*operands)


def piece_kernel(parts, out):
    total = parts[0].astype(f32)
    for k in range(1, parts.shape[0]):
        total += parts[k].astype(f32)
    share = out.shape[1]
    for k in range(out.shape[0]):
        out[k] = total[0:share] if k % 2 == 0 else total[share : 2 * share]


def add_pieces(parts):
    count, rows, rank = parts.shape
    return pl.pallas_call(
        piece_kernel,
        out_shape=jax.ShapeDtypeStruct((count, rows // 2, rank), f32),
        name="pieces", compiler_params=pltpu.CompilerParams(vmem_limit_bytes=6 << 20),
    )(parts)


def project_kernel(near, far, tiles, usable, out, flipped, gram):
    half, rank = near.shape
    band = gram.shape[0] // lax.axis_size("cols")

    @pl.when(pl.program_id(0) == 0)
    def _():
        contract = (((0,), (0,)), ((), ()))
        total = jnp.zeros_like(gram)
        cross = jnp.zeros_like(gram)
        for k, ref in enumerate((near, far)):
            whole = ref[...]
            upper = whole.astype(bf16)
            lower = (whole - upper.astype(f32)).astype(bf16)
            turned = upper.astype(f32).T.astype(bf16)
            flipped[:, half * k : half * (k + 1)] = turned
            cross += jnp.dot(turned, lower, preferred_element_type=f32)
            total += lax.dot_general(lower, lower, contract, preferred_element_type=f32)
            total += jnp.dot(turned, upper, preferred_element_type=f32)
        gram[...] = total + (cross + cross.T)

    product = jnp.dot(flipped[...], tiles[...], preferred_element_type=f32)
    product = (product * usable[...]).astype(bf16)
    first = pl.multiple_of(lax.axis_index("cols") * band, band)
    own = jnp.concatenate([part.astype(f32) for part in thirds(gram[pl.ds(first, band), :])], axis=0)
    own = own.astype(bf16)
    for k in range(out.shape[0]):
        out[k, 0:rank, :] = product[:, 128 * k : 128 * k + 128]
        out[k, rank:, :] = own


def project(near, far, tiles, usable, row_devices):
    nrows, ncols = tiles.shape
    half, rank = near.shape
    width = 512
    dests = width // (ncols // row_devices)
    return pl.pallas_call(
        project_kernel,
        grid=(ncols // width,),
        in_specs=[
            pl.BlockSpec((half, rank), lambda j: (0, 0), pipeline_mode=pl.Buffered(1)),
            pl.BlockSpec((half, rank), lambda j: (0, 0), pipeline_mode=pl.Buffered(1)),
            pl.BlockSpec((nrows, width), lambda j: (0, j)),
            pl.BlockSpec((1, width), lambda j: (0, j)),
        ],
        out_specs=pl.BlockSpec((dests, rank + 24, 128), lambda j: (j, 0, 0)),
        out_shape=jax.ShapeDtypeStruct((row_devices, rank + 24, 128), bf16),
        scratch_shapes=[pltpu.VMEM((rank, nrows), bf16), pltpu.VMEM((rank, rank), f32)],
        name="project", compiler_params=pltpu.CompilerParams(vmem_limit_bytes=14 << 20),
    )(near, far, tiles, usable)


def fold_kernel(parts, product, band):
    total = parts[0].astype(f32)
    for k in range(1, parts.shape[0]):
        total += parts[k].astype(f32)
    rank = product.shape[0]
    rows = band.shape[1]
    product[...] = total[0:rank]
    own = total[rank : rank + rows] + (
        total[rank + rows : rank + 2 * rows] + total[rank + 2 * rows : rank + 3 * rows]
    )
    for k in range(band.shape[0]):
        band[k] = own


def fold(parts, col_devices):
    rank = parts.shape[1] - 24
    return pl.pallas_call(
        fold_kernel,
        out_shape=[
            jax.ShapeDtypeStruct((rank, rank), f32),
            jax.ShapeDtypeStruct((col_devices, rank // col_devices, rank), f32),
        ],
        name="fold", compiler_params=pltpu.CompilerParams(vmem_limit_bytes=6 << 20),
    )(parts)


def inverse_factor(bands):
    count, _, rank = bands.shape
    shape = (8, rank)
    at_row = lax.broadcasted_iota(jnp.int32, shape, 0)
    at_col = lax.broadcasted_iota(jnp.int32, shape, 1)
    left = [bands[i] for i in range(count)]
    right = [jnp.where(at_col == at_row + 8 * i, 1.0, 0.0) for i in range(count)]
    inside = at_row < 8

    def along_lanes(values, k):
        return jnp.where(inside, jnp.broadcast_to(values[:, k : k + 1], shape), 0.0)

    def along_rows(values, r):
        return jnp.broadcast_to(values[r : r + 1, :], shape)

    for k in range(0, rank, 2):
        block, r = divmod(k, 8)
        first = [along_lanes(left[i], k) for i in range(block, count)]
        second = [along_lanes(left[i], k + 1) for i in range(block, count)]
        a, b, c = along_rows(first[0], r), along_rows(first[0], r + 1), along_rows(second[0], r + 1)
        scale = 1.0 / (a * c - b * b)
        a_s, b_s, c_s = a * scale, b * scale, c * scale
        upper, lower = along_rows(left[block], r), along_rows(left[block], r + 1)
        upper_r, lower_r = along_rows(right[block], r), along_rows(right[block], r + 1)
        for i in range(block, count):
            if i == block and r == 6:
                continue
            one, two = first[i - block], second[i - block]
            u = one * c_s - two * b_s
            v = two * a_s - one * b_s
            if i == block:
                u = jnp.where(at_row > r + 1, u, 0.0)
                v = jnp.where(at_row > r + 1, v, 0.0)
            left[i] = left[i] - (u * upper + v * lower)
            right[i] = right[i] - (u * upper_r + v * lower_r)
        ratio = jnp.where(at_row == r + 1, b * (1.0 / a), 0.0)
        left[block] = left[block] - ratio * upper
        right[block] = right[block] - ratio * upper_r
    out = []
    for i in range(count):
        diagonal = jnp.sum(jnp.where(at_col == at_row + 8 * i, left[i], 0.0), axis=1, keepdims=True)
        out.append(right[i] * lax.rsqrt(jnp.broadcast_to(diagonal, shape)))
    return out


def finish_kernel(scale, near, far, product, bands, basis, projected, inverse):
    for i, rows in enumerate(inverse_factor(bands)):
        inverse[8 * i : 8 * i + 8, :] = rows
    contract = (((1,), (1,)), ((), ()))
    high, middle, low = thirds(inverse[...] * scale)
    count = bands.shape[0]
    share = near.shape[0] // count
    for ref, keeper in zip((near, far), halves()):
        whole = ref[...]
        upper = whole.astype(bf16)
        lower = (whole - upper.astype(f32)).astype(bf16)
        total = lax.dot_general(upper, low, contract, preferred_element_type=f32)
        total += lax.dot_general(lower, middle, contract, preferred_element_type=f32)
        total += lax.dot_general(lower, high, contract, preferred_element_type=f32)
        total += lax.dot_general(upper, middle, contract, preferred_element_type=f32)
        total += lax.dot_general(upper, high, contract, preferred_element_type=f32)
        for k in range(count):
            rows = pl.ds(pl.multiple_of(share * (2 * k + keeper), share), share)
            basis[rows, :] = total[share * k : share * (k + 1)]
    projected[...] = lax.dot_general(
        product[...].T,
        inverse[...],
        contract,
        precision=lax.Precision.HIGHEST,
        preferred_element_type=f32,
    )


def finish(near, far, product, bands, scale):
    return pl.pallas_call(
        functools.partial(finish_kernel, scale),
        out_shape=[
            jax.ShapeDtypeStruct((2 * near.shape[0], near.shape[1]), f32),
            jax.ShapeDtypeStruct(product.shape, f32),
        ],
        scratch_shapes=[pltpu.VMEM(product.shape, f32)],
        name="finish", compiler_params=pltpu.CompilerParams(vmem_limit_bytes=8 << 20),
    )(near, far, product, bands)


def shards(targets, sources, weights, counts, omega):
    rows_here, cols_here, rank = targets.shape[1], sources.shape[1], omega.shape[1]
    row_devices, col_devices = lax.axis_size("rows"), lax.axis_size("cols")
    tiles, partial, usable = make_sketch(
        targets, sources, weights.reshape(1, -1), counts.reshape(1, -1), omega, col_devices
    )
    pieces = lax.all_to_all(partial, "cols", 0, 0)
    near = lax.all_to_all(add_pieces(pieces), "cols", 0, 0).reshape(rows_here // 2, rank)
    far = lax.ppermute(near, "cols", [(c, c ^ 1) for c in range(col_devices)])
    terms = lax.all_to_all(project(near, far, tiles, usable, row_devices), "rows", 0, 0)
    product, band = fold(terms, col_devices)
    bands = lax.all_to_all(band, "cols", 0, 0)
    return finish(near, far, product, bands, math.sqrt(rows_here * row_devices))


def solution(mesh):
    return jax.shard_map(
        shards,
        mesh=mesh,
        in_specs=(P(None, "rows"), P(None, "cols"), P("cols"), P("cols"), P("cols", None)),
        out_specs=(P("rows", None), P(("cols", "rows"), None)),
        check_vma=False,
    )
```

```python
import functools
import math

import jax
import jax.numpy as jnp
from jax import lax
from jax.experimental import pallas as pl
from jax.experimental.pallas import tpu as pltpu
from jax.sharding import PartitionSpec as P

f32 = jnp.float32
bf16 = jnp.bfloat16
wave_number = 160.0
separation = 2.0
turns = wave_number / (2.0 * math.pi)
sine = (6.283164043875678, -41.33714231633244, 81.34076713243772, -70.99341720807224)
target_tile = 1024
source_tile = 512


def thirds(values):
    high = values.astype(bf16)
    rest = values - high.astype(f32)
    middle = rest.astype(bf16)
    low = (rest - middle.astype(f32)).astype(bf16)
    return high, middle, low


def pick_rows(rows, shape):
    at = lax.broadcasted_iota(jnp.int32, shape, 0)
    out = jnp.zeros(shape, f32)
    for k, row in enumerate(rows):
        out = jnp.where(at == k, jnp.broadcast_to(row, shape), out)
    return out


def put_thirds(ref, values, outer):
    parts = [part.astype(f32) for part in thirds(values)]
    for p in range(3):
        for q in range(3):
            k = 3 * p + q
            ref[8 * k : 8 * k + 8, :] = parts[p if outer else q]


def halves():
    own = lax.rem(lax.axis_index("cols"), 2)
    return own, 1 - own


def sketch_kernel(targets_in, sources_in, weights_in, counts_in, omega_in, tiles, sketch, usable,
                  targets, sources, weights, counts, omega, arrived, feature, tfeat, afeat, bfeat, masked, k_even, k_odd, acc):
    step = pl.program_id(0)
    nrows, ncols = targets.shape[1], sources.shape[1]
    per_step = nrows // target_tile
    total = per_step * (ncols // source_tile)

    def block(at, size):
        return pl.ds(pl.multiple_of(at * size, size), size)

    def accumulate(tile, k_buf):
        rows = block(lax.rem(tile, per_step), target_tile)
        there = block(lax.div(tile, per_step), source_tile)
        acc[rows, :] += jnp.dot(k_buf[...], masked[there, :], preferred_element_type=f32)

    own, other = halves()
    half = nrows // 2
    pieces, rank = sketch.shape[0], sketch.shape[2]
    share = half // pieces

    @pl.when(step == 0)
    def _():
        moves = [
            pltpu.make_async_copy(source, target, arrived.at[k])
            for k, (source, target) in enumerate(
                [(targets_in, targets), (sources_in, sources), (weights_in, weights), (counts_in, counts), (omega_in, omega)]
            )
        ]
        for move in moves:
            move.start()
        feature[...] = jnp.zeros_like(feature)
        moves[0].wait()
        tx = (targets[0:1, :] - (0.5 + 0.5 * separation)) * turns
        ty = (targets[1:2, :] - 0.5) * turns
        tz = (targets[2:3, :] - 0.5) * turns
        rows = [tx, ty, tz, tx * tx + ty * ty + tz * tz, jnp.ones_like(tx)]
        view = feature.at[:, 0:nrows]
        put_thirds(view, pick_rows(rows, (8, nrows)), True)
        for k in range(pieces):
            block_rows = feature[:, 2 * share * k : 2 * share * (k + 1)].T.astype(bf16)
            tfeat[pl.ds(pl.multiple_of(own * half + share * k, share), share), :] = block_rows[0:share]
            tfeat[pl.ds(pl.multiple_of(other * half + share * k, share), share), :] = block_rows[share : 2 * share]
        for move in moves[1:4]:
            move.wait()
        sx = (sources[0:1, :] + (0.5 * separation - 0.5)) * turns
        sy = (sources[1:2, :] - 0.5) * turns
        sz = (sources[2:3, :] - 0.5) * turns
        norm = sx * sx + sy * sy + sz * sz
        inverse = (1.0 / (-sine[3] * turns)) / weights[...]
        for ref, scale in ((bfeat, inverse), (afeat, inverse * inverse)):
            rows = [-2.0 * sx * scale, -2.0 * sy * scale, -2.0 * sz * scale, scale, norm * scale]
            put_thirds(feature, pick_rows(rows, (8, ncols)), False)
            ref[...] = feature[...].astype(bf16)
        panels = counts.shape[1]
        size = ncols // panels
        span = 128 // size
        shape = (ncols // 128, panels)
        mine = lax.shift_right_logical(lax.broadcasted_iota(jnp.int32, shape, 1), span.bit_length() - 1) == lax.broadcasted_iota(jnp.int32, shape, 0)
        chosen = jnp.where(mine, jnp.broadcast_to(counts[...].astype(f32), shape), 0.0).astype(bf16)
        shape = (panels, 128)
        spread = (lax.broadcasted_iota(jnp.int32, shape, 0) & (span - 1)) == lax.shift_right_logical(lax.broadcasted_iota(jnp.int32, shape, 1), size.bit_length() - 1)
        filled = jnp.dot(chosen, jnp.where(spread, 1.0, 0.0).astype(bf16), preferred_element_type=f32)
        lane = (lax.broadcasted_iota(jnp.int32, filled.shape, 1) & (size - 1)).astype(f32)
        flags = jnp.where(lane < filled, 1.0, 0.0)
        for k in range(ncols // 128):
            usable[0:1, 128 * k : 128 * k + 128] = flags[k : k + 1, :]
        moves[4].wait()
        columns = flags.T
        for k in range(ncols // 128):
            rows = slice(128 * k, 128 * k + 128)
            flag = jnp.broadcast_to(columns[:, k : k + 1], (128, rank))
            masked[rows, :] = (omega[rows, :].astype(f32) * flag).astype(bf16)
        acc[...] = jnp.zeros_like(acc)
        k_odd[...] = jnp.zeros_like(k_odd)

    def pair(p, carry):
        for odd, (k_now, k_last) in enumerate(((k_even, k_odd), (k_odd, k_even))):
            tile = step * per_step + 2 * p + odd
            there = block(lax.div(tile, per_step), source_tile)
            for part in range(target_tile // 256):
                at = block(lax.rem(tile, per_step) * (target_tile // 256) + part, 256)
                over = lax.rsqrt(jnp.dot(tfeat[at, :], afeat[:, there], preferred_element_type=f32))
                turn = jnp.dot(tfeat[at, :], bfeat[:, there], preferred_element_type=f32) * over
                away = jnp.abs(turn - jnp.round(turn)) - 0.25
                square = away * away
                wave = ((square + sine[2] / sine[3]) * square + sine[1] / sine[3]) * square + sine[0] / sine[3]
                low = ((wave * away) * over).astype(bf16)
                k_now[256 * part : 256 * (part + 1), :] = low
                tiles[at, :] = low
            accumulate(jnp.maximum(tile - 1, 0), k_last)
        return carry

    lax.fori_loop(0, per_step // 2, pair, 0)

    @pl.when(step == pl.num_programs(0) - 1)
    def _():
        accumulate(total - 1, k_odd)
        for k in range(pieces):
            for part, keeper in ((0, own), (1, other)):
                rows = pl.ds(pl.multiple_of(keeper * half + share * k, share), share)
                sketch[k, part * share : (part + 1) * share, :] = acc[rows, :].astype(bf16)


def make_sketch(targets, sources, weights, counts, omega, col_devices):
    nrows, ncols, rank = targets.shape[1], sources.shape[1], omega.shape[1]
    operands = [pltpu.with_memory_space_constraint(x, pltpu.HBM) for x in (targets, sources, weights, counts, omega)]
    return pl.pallas_call(
        sketch_kernel,
        grid=(ncols // source_tile,),
        in_specs=[pl.BlockSpec(memory_space=pltpu.HBM)] * 5,
        out_specs=[
            pl.BlockSpec((nrows, source_tile), lambda j: (0, j)),
            pl.BlockSpec((col_devices, nrows // col_devices, rank), lambda j: (0, 0, 0)),
            pl.BlockSpec((1, ncols), lambda j: (0, 0)),
        ],
        out_shape=[
            jax.ShapeDtypeStruct((nrows, ncols), bf16),
            jax.ShapeDtypeStruct((col_devices, nrows // col_devices, rank), bf16),
            jax.ShapeDtypeStruct((1, ncols), f32),
        ],
        scratch_shapes=[
            pltpu.VMEM((3, nrows), f32),
            pltpu.VMEM((3, ncols), f32),
            pltpu.VMEM((1, ncols), f32),
            pltpu.VMEM(counts.shape, jnp.int32),
            pltpu.VMEM((ncols, rank), bf16),
            pltpu.SemaphoreType.DMA((5,)),
            pltpu.VMEM((128, ncols), f32),
            pltpu.VMEM((nrows, 128), bf16),
            pltpu.VMEM((128, ncols), bf16),
            pltpu.VMEM((128, ncols), bf16),
            pltpu.VMEM((ncols, rank), bf16),
            pltpu.VMEM((target_tile, source_tile), bf16),
            pltpu.VMEM((target_tile, source_tile), bf16),
            pltpu.VMEM((nrows, rank), f32),
        ],
        name="sketch", compiler_params=pltpu.CompilerParams(vmem_limit_bytes=24 << 20),
    )(*operands)


def piece_kernel(parts, out):
    total = parts[0].astype(f32)
    for k in range(1, parts.shape[0]):
        total += parts[k].astype(f32)
    share = out.shape[1]
    for k in range(out.shape[0]):
        out[k] = total[0:share] if k % 2 == 0 else total[share : 2 * share]


def add_pieces(parts):
    count, rows, rank = parts.shape
    return pl.pallas_call(
        piece_kernel,
        out_shape=jax.ShapeDtypeStruct((count, rows // 2, rank), f32),
        name="pieces", compiler_params=pltpu.CompilerParams(vmem_limit_bytes=6 << 20),
    )(parts)


def project_kernel(near, far, tiles, usable, out, flipped, gram):
    half, rank = near.shape
    band = gram.shape[0] // lax.axis_size("cols")

    @pl.when(pl.program_id(0) == 0)
    def _():
        contract = (((0,), (0,)), ((), ()))
        total = jnp.zeros_like(gram)
        cross = jnp.zeros_like(gram)
        for k, ref in enumerate((near, far)):
            whole = ref[...]
            upper = whole.astype(bf16)
            lower = (whole - upper.astype(f32)).astype(bf16)
            turned = upper.astype(f32).T.astype(bf16)
            flipped[:, half * k : half * (k + 1)] = turned
            cross += jnp.dot(turned, lower, preferred_element_type=f32)
            total += lax.dot_general(lower, lower, contract, preferred_element_type=f32)
            total += jnp.dot(turned, upper, preferred_element_type=f32)
        gram[...] = total + (cross + cross.T)

    product = jnp.dot(flipped[...], tiles[...], preferred_element_type=f32)
    product = (product * usable[...]).astype(bf16)
    first = pl.multiple_of(lax.axis_index("cols") * band, band)
    own = jnp.concatenate([part.astype(f32) for part in thirds(gram[pl.ds(first, band), :])[0:2]], axis=0)
    own = own.astype(bf16)
    for k in range(out.shape[0]):
        out[k, 0:rank, :] = product[:, 128 * k : 128 * k + 128]
        out[k, rank:, :] = own


def project(near, far, tiles, usable, row_devices):
    nrows, ncols = tiles.shape
    half, rank = near.shape
    width = 512
    dests = width // (ncols // row_devices)
    return pl.pallas_call(
        project_kernel,
        grid=(ncols // width,),
        in_specs=[
            pl.BlockSpec((half, rank), lambda j: (0, 0), pipeline_mode=pl.Buffered(1)),
            pl.BlockSpec((half, rank), lambda j: (0, 0), pipeline_mode=pl.Buffered(1)),
            pl.BlockSpec((nrows, width), lambda j: (0, j)),
            pl.BlockSpec((1, width), lambda j: (0, j)),
        ],
        out_specs=pl.BlockSpec((dests, rank + 16, 128), lambda j: (j, 0, 0)),
        out_shape=jax.ShapeDtypeStruct((row_devices, rank + 16, 128), bf16),
        scratch_shapes=[pltpu.VMEM((rank, nrows), bf16), pltpu.VMEM((rank, rank), f32)],
        name="project", compiler_params=pltpu.CompilerParams(vmem_limit_bytes=14 << 20),
    )(near, far, tiles, usable)


def fold_kernel(parts, product, band):
    total = parts[0].astype(f32)
    for k in range(1, parts.shape[0]):
        total += parts[k].astype(f32)
    rank = product.shape[0]
    rows = band.shape[1]
    product[...] = total[0:rank]
    own = total[rank : rank + rows] + total[rank + rows : rank + 2 * rows]
    for k in range(band.shape[0]):
        band[k] = own


def fold(parts, col_devices):
    rank = parts.shape[1] - 16
    return pl.pallas_call(
        fold_kernel,
        out_shape=[
            jax.ShapeDtypeStruct((rank, rank), f32),
            jax.ShapeDtypeStruct((col_devices, rank // col_devices, rank), f32),
        ],
        name="fold", compiler_params=pltpu.CompilerParams(vmem_limit_bytes=6 << 20),
    )(parts)


def inverse_factor(bands):
    count, _, rank = bands.shape
    shape = (8, rank)
    at_row = lax.broadcasted_iota(jnp.int32, shape, 0)
    at_col = lax.broadcasted_iota(jnp.int32, shape, 1)
    left = [bands[i] for i in range(count)]
    right = [jnp.where(at_col == at_row + 8 * i, 1.0, 0.0) for i in range(count)]
    inside = at_row < 8

    def along_lanes(values, k):
        return jnp.where(inside, jnp.broadcast_to(values[:, k : k + 1], shape), 0.0)

    def along_rows(values, r):
        return jnp.broadcast_to(values[r : r + 1, :], shape)

    for k in range(0, rank, 2):
        block, r = divmod(k, 8)
        first = [along_lanes(left[i], k) for i in range(block, count)]
        second = [along_lanes(left[i], k + 1) for i in range(block, count)]
        a, b, c = along_rows(first[0], r), along_rows(first[0], r + 1), along_rows(second[0], r + 1)
        scale = 1.0 / (a * c - b * b)
        a_s, b_s, c_s = a * scale, b * scale, c * scale
        upper, lower = along_rows(left[block], r), along_rows(left[block], r + 1)
        upper_r, lower_r = along_rows(right[block], r), along_rows(right[block], r + 1)
        for i in range(block, count):
            if i == block and r == 6:
                continue
            one, two = first[i - block], second[i - block]
            u = one * c_s - two * b_s
            v = two * a_s - one * b_s
            if i == block:
                u = jnp.where(at_row > r + 1, u, 0.0)
                v = jnp.where(at_row > r + 1, v, 0.0)
            left[i] = left[i] - (u * upper + v * lower)
            right[i] = right[i] - (u * upper_r + v * lower_r)
        ratio = jnp.where(at_row == r + 1, b * (1.0 / a), 0.0)
        left[block] = left[block] - ratio * upper
        right[block] = right[block] - ratio * upper_r
    out = []
    for i in range(count):
        diagonal = jnp.sum(jnp.where(at_col == at_row + 8 * i, left[i], 0.0), axis=1, keepdims=True)
        out.append(right[i] * lax.rsqrt(jnp.broadcast_to(diagonal, shape)))
    return out


def finish_kernel(scale, near_in, far_in, product, bands, basis, projected, inverse, near, far, arrived):
    moves = [
        pltpu.make_async_copy(near_in, near, arrived.at[0]),
        pltpu.make_async_copy(far_in, far, arrived.at[1]),
    ]
    for move in moves:
        move.start()
    for i, rows in enumerate(inverse_factor(bands)):
        inverse[8 * i : 8 * i + 8, :] = rows
    contract = (((1,), (1,)), ((), ()))
    high, middle, low = thirds(inverse[...] * scale)
    for move in moves:
        move.wait()
    count = bands.shape[0]
    share = near.shape[0] // count
    for ref, keeper in zip((near, far), halves()):
        whole = ref[...]
        upper = whole.astype(bf16)
        lower = (whole - upper.astype(f32)).astype(bf16)
        total = lax.dot_general(upper, low, contract, preferred_element_type=f32)
        total += lax.dot_general(lower, middle, contract, preferred_element_type=f32)
        total += lax.dot_general(lower, high, contract, preferred_element_type=f32)
        total += lax.dot_general(upper, middle, contract, preferred_element_type=f32)
        total += lax.dot_general(upper, high, contract, preferred_element_type=f32)
        for k in range(count):
            rows = pl.ds(pl.multiple_of(share * (2 * k + keeper), share), share)
            basis[rows, :] = total[share * k : share * (k + 1)]
    projected[...] = lax.dot_general(
        product[...].T,
        inverse[...],
        contract,
        precision=lax.Precision.HIGHEST,
        preferred_element_type=f32,
    )


def finish(near, far, product, bands, scale):
    return pl.pallas_call(
        functools.partial(finish_kernel, scale),
        out_shape=[
            jax.ShapeDtypeStruct((2 * near.shape[0], near.shape[1]), f32),
            jax.ShapeDtypeStruct(product.shape, f32),
        ],
        in_specs=[
            pl.BlockSpec(memory_space=pl.ANY),
            pl.BlockSpec(memory_space=pl.ANY),
            pl.BlockSpec(memory_space=pltpu.VMEM),
            pl.BlockSpec(memory_space=pltpu.VMEM),
        ],
        scratch_shapes=[
            pltpu.VMEM(product.shape, f32),
            pltpu.VMEM(near.shape, f32),
            pltpu.VMEM(far.shape, f32),
            pltpu.SemaphoreType.DMA((2,)),
        ],
        name="finish", compiler_params=pltpu.CompilerParams(vmem_limit_bytes=8 << 20),
    )(near, far, product, bands)


def shards(targets, sources, weights, counts, omega):
    rows_here, cols_here, rank = targets.shape[1], sources.shape[1], omega.shape[1]
    row_devices, col_devices = lax.axis_size("rows"), lax.axis_size("cols")
    tiles, partial, usable = make_sketch(
        targets, sources, weights.reshape(1, -1), counts.reshape(1, -1), omega, col_devices
    )
    pieces = lax.all_to_all(partial, "cols", 0, 0)
    near = lax.all_to_all(add_pieces(pieces), "cols", 0, 0).reshape(rows_here // 2, rank)
    far = lax.ppermute(near, "cols", [(c, c ^ 1) for c in range(col_devices)])
    terms = lax.all_to_all(project(near, far, tiles, usable, row_devices), "rows", 0, 0)
    product, band = fold(terms, col_devices)
    bands = lax.all_to_all(band, "cols", 0, 0)
    return finish(near, far, product, bands, math.sqrt(rows_here * row_devices))


def solution(mesh):
    return jax.shard_map(
        shards,
        mesh=mesh,
        in_specs=(P(None, "rows"), P(None, "cols"), P("cols"), P("cols"), P("cols", None)),
        out_specs=(P("rows", None), P(("cols", "rows"), None)),
        check_vma=False,
    )
```

```python
import functools
import math

import jax
import jax.numpy as jnp
from jax import lax
from jax.experimental import pallas as pl
from jax.experimental.pallas import tpu as pltpu
from jax.sharding import PartitionSpec as P

f32 = jnp.float32
bf16 = jnp.bfloat16
wave_number = 160.0
separation = 2.0
turns = wave_number / (2.0 * math.pi)
sine = (6.283164043875678, -41.33714231633244, 81.34076713243772, -70.99341720807224)
target_tile = 1024
source_tile = 512


def thirds(values):
    high = values.astype(bf16)
    rest = values - high.astype(f32)
    middle = rest.astype(bf16)
    low = (rest - middle.astype(f32)).astype(bf16)
    return high, middle, low


def pick_rows(rows, shape):
    at = lax.broadcasted_iota(jnp.int32, shape, 0)
    out = jnp.zeros(shape, f32)
    for k, row in enumerate(rows):
        out = jnp.where(at == k, jnp.broadcast_to(row, shape), out)
    return out


def put_thirds(ref, values, outer):
    parts = [part.astype(f32) for part in thirds(values)]
    for p in range(3):
        for q in range(3):
            k = 3 * p + q
            ref[8 * k : 8 * k + 8, :] = parts[p if outer else q]


def halves():
    own = lax.rem(lax.axis_index("cols"), 2)
    return own, 1 - own


def sketch_kernel(targets_in, sources_in, weights_in, counts_in, omega_in, tiles, sketch, usable,
                  targets, sources, weights, counts, omega, arrived, feature, tfeat, afeat, bfeat, masked, k_even, k_odd, acc):
    step = pl.program_id(0)
    nrows, ncols = targets.shape[1], sources.shape[1]
    per_step = nrows // target_tile
    total = per_step * (ncols // source_tile)

    def block(at, size):
        return pl.ds(pl.multiple_of(at * size, size), size)

    def accumulate(tile, k_buf):
        rows = block(lax.rem(tile, per_step), target_tile)
        there = block(lax.div(tile, per_step), source_tile)
        acc[rows, :] += jnp.dot(k_buf[...], masked[there, :], preferred_element_type=f32)

    own, other = halves()
    half = nrows // 2
    pieces, rank = sketch.shape[0], sketch.shape[2]
    share = half // pieces

    @pl.when(step == 0)
    def _():
        moves = [
            pltpu.make_async_copy(source, target, arrived.at[k])
            for k, (source, target) in enumerate(
                [(targets_in, targets), (sources_in, sources), (weights_in, weights), (counts_in, counts), (omega_in, omega)]
            )
        ]
        for move in moves:
            move.start()
        feature[72:80, :] = jnp.zeros((8, ncols), f32)
        moves[0].wait()
        tx = (targets[0:1, :] - (0.5 + 0.5 * separation)) * turns
        ty = (targets[1:2, :] - 0.5) * turns
        tz = (targets[2:3, :] - 0.5) * turns
        rows = [tx, ty, tz, tx * tx + ty * ty + tz * tz, jnp.ones_like(tx)]
        view = feature.at[:, 0:nrows]
        put_thirds(view, pick_rows(rows, (8, nrows)), True)
        for k in range(pieces):
            block_rows = feature[:, 2 * share * k : 2 * share * (k + 1)].T.astype(bf16)
            tfeat[pl.ds(pl.multiple_of(own * half + share * k, share), share), :] = block_rows[0:share]
            tfeat[pl.ds(pl.multiple_of(other * half + share * k, share), share), :] = block_rows[share : 2 * share]
        for move in moves[1:4]:
            move.wait()
        sx = (sources[0:1, :] + (0.5 * separation - 0.5)) * turns
        sy = (sources[1:2, :] - 0.5) * turns
        sz = (sources[2:3, :] - 0.5) * turns
        norm = sx * sx + sy * sy + sz * sz
        inverse = (1.0 / (-sine[3] * turns)) / weights[...]
        for ref, scale in ((bfeat, inverse), (afeat, inverse * inverse)):
            rows = [-2.0 * sx * scale, -2.0 * sy * scale, -2.0 * sz * scale, scale, norm * scale]
            put_thirds(feature, pick_rows(rows, (8, ncols)), False)
            ref[...] = feature[...].astype(bf16)
        panels = counts.shape[1]
        size = ncols // panels
        span = 128 // size
        shape = (ncols // 128, panels)
        mine = lax.shift_right_logical(lax.broadcasted_iota(jnp.int32, shape, 1), span.bit_length() - 1) == lax.broadcasted_iota(jnp.int32, shape, 0)
        chosen = jnp.where(mine, jnp.broadcast_to(counts[...].astype(f32), shape), 0.0).astype(bf16)
        shape = (panels, 128)
        spread = (lax.broadcasted_iota(jnp.int32, shape, 0) & (span - 1)) == lax.shift_right_logical(lax.broadcasted_iota(jnp.int32, shape, 1), size.bit_length() - 1)
        filled = jnp.dot(chosen, jnp.where(spread, 1.0, 0.0).astype(bf16), preferred_element_type=f32)
        lane = (lax.broadcasted_iota(jnp.int32, filled.shape, 1) & (size - 1)).astype(f32)
        flags = jnp.where(lane < filled, 1.0, 0.0)
        for k in range(ncols // 128):
            usable[0:1, 128 * k : 128 * k + 128] = flags[k : k + 1, :]
        moves[4].wait()
        columns = flags.T
        for k in range(ncols // 128):
            rows = slice(128 * k, 128 * k + 128)
            flag = jnp.broadcast_to(columns[:, k : k + 1], (128, rank))
            masked[rows, :] = (omega[rows, :].astype(f32) * flag).astype(bf16)
        acc[...] = jnp.zeros_like(acc)
        k_odd[...] = jnp.zeros_like(k_odd)

    def pair(p, carry):
        for odd, (k_now, k_last) in enumerate(((k_even, k_odd), (k_odd, k_even))):
            tile = step * per_step + 2 * p + odd
            there = block(lax.div(tile, per_step), source_tile)
            for part in range(target_tile // 256):
                at = block(lax.rem(tile, per_step) * (target_tile // 256) + part, 256)
                over = lax.rsqrt(jnp.dot(tfeat[at, :], afeat[:, there], preferred_element_type=f32))
                turn = jnp.dot(tfeat[at, :], bfeat[:, there], preferred_element_type=f32) * over
                away = jnp.abs(turn - jnp.round(turn)) - 0.25
                square = away * away
                wave = ((square + sine[2] / sine[3]) * square + sine[1] / sine[3]) * square + sine[0] / sine[3]
                low = ((wave * away) * over).astype(bf16)
                k_now[256 * part : 256 * (part + 1), :] = low
                tiles[at, :] = low
            accumulate(jnp.maximum(tile - 1, 0), k_last)
        return carry

    lax.fori_loop(0, per_step // 2, pair, 0)

    @pl.when(step == pl.num_programs(0) - 1)
    def _():
        accumulate(total - 1, k_odd)
        for k in range(pieces):
            for part, keeper in ((0, own), (1, other)):
                rows = pl.ds(pl.multiple_of(keeper * half + share * k, share), share)
                sketch[k, part * share : (part + 1) * share, :] = acc[rows, :].astype(bf16)


def make_sketch(targets, sources, weights, counts, omega, col_devices):
    nrows, ncols, rank = targets.shape[1], sources.shape[1], omega.shape[1]
    operands = [pltpu.with_memory_space_constraint(x, pltpu.HBM) for x in (targets, sources, weights, counts, omega)]
    return pl.pallas_call(
        sketch_kernel,
        grid=(ncols // source_tile,),
        in_specs=[pl.BlockSpec(memory_space=pltpu.HBM)] * 5,
        out_specs=[
            pl.BlockSpec((nrows, source_tile), lambda j: (0, j)),
            pl.BlockSpec((col_devices, nrows // col_devices, rank), lambda j: (0, 0, 0)),
            pl.BlockSpec((1, ncols), lambda j: (0, 0)),
        ],
        out_shape=[
            jax.ShapeDtypeStruct((nrows, ncols), bf16),
            jax.ShapeDtypeStruct((col_devices, nrows // col_devices, rank), bf16),
            jax.ShapeDtypeStruct((1, ncols), f32),
        ],
        scratch_shapes=[
            pltpu.VMEM((3, nrows), f32),
            pltpu.VMEM((3, ncols), f32),
            pltpu.VMEM((1, ncols), f32),
            pltpu.VMEM(counts.shape, jnp.int32),
            pltpu.VMEM((ncols, rank), bf16),
            pltpu.SemaphoreType.DMA((5,)),
            pltpu.VMEM((80, ncols), f32),
            pltpu.VMEM((nrows, 80), bf16),
            pltpu.VMEM((80, ncols), bf16),
            pltpu.VMEM((80, ncols), bf16),
            pltpu.VMEM((ncols, rank), bf16),
            pltpu.VMEM((target_tile, source_tile), bf16),
            pltpu.VMEM((target_tile, source_tile), bf16),
            pltpu.VMEM((nrows, rank), f32),
        ],
        name="sketch", compiler_params=pltpu.CompilerParams(vmem_limit_bytes=24 << 20),
    )(*operands)


def piece_kernel(parts, out):
    total = parts[0].astype(f32)
    for k in range(1, parts.shape[0]):
        total += parts[k].astype(f32)
    share = out.shape[1]
    for k in range(out.shape[0]):
        out[k] = total[0:share] if k % 2 == 0 else total[share : 2 * share]


def add_pieces(parts):
    count, rows, rank = parts.shape
    return pl.pallas_call(
        piece_kernel,
        out_shape=jax.ShapeDtypeStruct((count, rows // 2, rank), f32),
        name="pieces", compiler_params=pltpu.CompilerParams(vmem_limit_bytes=6 << 20),
    )(parts)


def project_kernel(near, far, tiles, usable, out, flipped, gram):
    half, rank = near.shape
    band = gram.shape[0] // lax.axis_size("cols")

    @pl.when(pl.program_id(0) == 0)
    def _():
        contract = (((0,), (0,)), ((), ()))
        total = jnp.zeros_like(gram)
        cross = jnp.zeros_like(gram)
        for k, ref in enumerate((near, far)):
            whole = ref[...]
            upper = whole.astype(bf16)
            lower = (whole - upper.astype(f32)).astype(bf16)
            turned = upper.astype(f32).T.astype(bf16)
            flipped[:, half * k : half * (k + 1)] = turned
            cross += jnp.dot(turned, lower, preferred_element_type=f32)
            total += lax.dot_general(lower, lower, contract, preferred_element_type=f32)
            total += jnp.dot(turned, upper, preferred_element_type=f32)
        gram[...] = total + (cross + cross.T)

    product = jnp.dot(flipped[...], tiles[...], preferred_element_type=f32)
    product = (product * usable[...]).astype(bf16)
    first = pl.multiple_of(lax.axis_index("cols") * band, band)
    own = jnp.concatenate([part.astype(f32) for part in thirds(gram[pl.ds(first, band), :])[0:2]], axis=0)
    own = own.astype(bf16)
    for k in range(out.shape[0]):
        out[k, 0:rank, :] = product[:, 128 * k : 128 * k + 128]
        out[k, rank:, :] = own


def project(near, far, tiles, usable, row_devices):
    nrows, ncols = tiles.shape
    half, rank = near.shape
    width = 512
    dests = width // (ncols // row_devices)
    return pl.pallas_call(
        project_kernel,
        grid=(ncols // width,),
        in_specs=[
            pl.BlockSpec((half, rank), lambda j: (0, 0), pipeline_mode=pl.Buffered(1)),
            pl.BlockSpec((half, rank), lambda j: (0, 0), pipeline_mode=pl.Buffered(1)),
            pl.BlockSpec((nrows, width), lambda j: (0, j)),
            pl.BlockSpec((1, width), lambda j: (0, j)),
        ],
        out_specs=pl.BlockSpec((dests, rank + 16, 128), lambda j: (j, 0, 0)),
        out_shape=jax.ShapeDtypeStruct((row_devices, rank + 16, 128), bf16),
        scratch_shapes=[pltpu.VMEM((rank, nrows), bf16), pltpu.VMEM((rank, rank), f32)],
        name="project", compiler_params=pltpu.CompilerParams(vmem_limit_bytes=14 << 20),
    )(near, far, tiles, usable)


def fold_kernel(parts, product, band):
    total = parts[0].astype(f32)
    for k in range(1, parts.shape[0]):
        total += parts[k].astype(f32)
    rank = product.shape[0]
    rows = band.shape[1]
    product[...] = total[0:rank]
    own = total[rank : rank + rows] + total[rank + rows : rank + 2 * rows]
    for k in range(band.shape[0]):
        band[k] = own


def fold(parts, col_devices):
    rank = parts.shape[1] - 16
    return pl.pallas_call(
        fold_kernel,
        out_shape=[
            jax.ShapeDtypeStruct((rank, rank), f32),
            jax.ShapeDtypeStruct((col_devices, rank // col_devices, rank), f32),
        ],
        name="fold", compiler_params=pltpu.CompilerParams(vmem_limit_bytes=6 << 20),
    )(parts)


def inverse_factor(bands):
    count, _, rank = bands.shape
    shape = (8, rank)
    at_row = lax.broadcasted_iota(jnp.int32, shape, 0)
    at_col = lax.broadcasted_iota(jnp.int32, shape, 1)
    left = [bands[i] for i in range(count)]
    right = [jnp.where(at_col == at_row + 8 * i, 1.0, 0.0) for i in range(count)]
    inside = at_row < 8

    def along_lanes(values, k):
        return jnp.where(inside, jnp.broadcast_to(values[:, k : k + 1], shape), 0.0)

    def along_rows(values, r):
        return jnp.broadcast_to(values[r : r + 1, :], shape)

    for k in range(0, rank, 2):
        block, r = divmod(k, 8)
        first = [along_lanes(left[i], k) for i in range(block, count)]
        second = [along_lanes(left[i], k + 1) for i in range(block, count)]
        a, b, c = along_rows(first[0], r), along_rows(first[0], r + 1), along_rows(second[0], r + 1)
        scale = 1.0 / (a * c - b * b)
        a_s, b_s, c_s = a * scale, b * scale, c * scale
        upper, lower = along_rows(left[block], r), along_rows(left[block], r + 1)
        upper_r, lower_r = along_rows(right[block], r), along_rows(right[block], r + 1)
        for i in range(block, count):
            if i == block and r == 6:
                continue
            one, two = first[i - block], second[i - block]
            u = one * c_s - two * b_s
            v = two * a_s - one * b_s
            if i == block:
                u = jnp.where(at_row > r + 1, u, 0.0)
                v = jnp.where(at_row > r + 1, v, 0.0)
            left[i] = left[i] - (u * upper + v * lower)
            right[i] = right[i] - (u * upper_r + v * lower_r)
        ratio = jnp.where(at_row == r + 1, b * (1.0 / a), 0.0)
        left[block] = left[block] - ratio * upper
        right[block] = right[block] - ratio * upper_r
    out = []
    for i in range(count):
        diagonal = jnp.sum(jnp.where(at_col == at_row + 8 * i, left[i], 0.0), axis=1, keepdims=True)
        out.append(right[i] * lax.rsqrt(jnp.broadcast_to(diagonal, shape)))
    return out


def finish_kernel(scale, near_in, far_in, product, bands, basis, projected, inverse, near, far, arrived):
    moves = [
        pltpu.make_async_copy(near_in, near, arrived.at[0]),
        pltpu.make_async_copy(far_in, far, arrived.at[1]),
    ]
    for move in moves:
        move.start()
    for i, rows in enumerate(inverse_factor(bands)):
        inverse[8 * i : 8 * i + 8, :] = rows
    contract = (((1,), (1,)), ((), ()))
    high, middle, low = thirds(inverse[...] * scale)
    for move in moves:
        move.wait()
    count = bands.shape[0]
    share = near.shape[0] // count
    for ref, keeper in zip((near, far), halves()):
        whole = ref[...]
        upper = whole.astype(bf16)
        lower = (whole - upper.astype(f32)).astype(bf16)
        total = lax.dot_general(upper, low, contract, preferred_element_type=f32)
        total += lax.dot_general(lower, middle, contract, preferred_element_type=f32)
        total += lax.dot_general(lower, high, contract, preferred_element_type=f32)
        total += lax.dot_general(upper, middle, contract, preferred_element_type=f32)
        total += lax.dot_general(upper, high, contract, preferred_element_type=f32)
        for k in range(count):
            rows = pl.ds(pl.multiple_of(share * (2 * k + keeper), share), share)
            basis[rows, :] = total[share * k : share * (k + 1)]
    projected[...] = lax.dot_general(
        product[...].T,
        inverse[...],
        contract,
        precision=lax.Precision.HIGHEST,
        preferred_element_type=f32,
    )


def finish(near, far, product, bands, scale):
    return pl.pallas_call(
        functools.partial(finish_kernel, scale),
        out_shape=[
            jax.ShapeDtypeStruct((2 * near.shape[0], near.shape[1]), f32),
            jax.ShapeDtypeStruct(product.shape, f32),
        ],
        in_specs=[
            pl.BlockSpec(memory_space=pl.ANY),
            pl.BlockSpec(memory_space=pl.ANY),
            pl.BlockSpec(memory_space=pltpu.VMEM),
            pl.BlockSpec(memory_space=pltpu.VMEM),
        ],
        scratch_shapes=[
            pltpu.VMEM(product.shape, f32),
            pltpu.VMEM(near.shape, f32),
            pltpu.VMEM(far.shape, f32),
            pltpu.SemaphoreType.DMA((2,)),
        ],
        name="finish", compiler_params=pltpu.CompilerParams(vmem_limit_bytes=8 << 20),
    )(near, far, product, bands)


def shards(targets, sources, weights, counts, omega):
    rows_here, cols_here, rank = targets.shape[1], sources.shape[1], omega.shape[1]
    row_devices, col_devices = lax.axis_size("rows"), lax.axis_size("cols")
    tiles, partial, usable = make_sketch(
        targets, sources, weights.reshape(1, -1), counts.reshape(1, -1), omega, col_devices
    )
    pieces = lax.all_to_all(partial, "cols", 0, 0)
    near = lax.all_to_all(add_pieces(pieces), "cols", 0, 0).reshape(rows_here // 2, rank)
    far = lax.ppermute(near, "cols", [(c, c ^ 1) for c in range(col_devices)])
    terms = lax.all_to_all(project(near, far, tiles, usable, row_devices), "rows", 0, 0)
    product, band = fold(terms, col_devices)
    bands = lax.all_to_all(band, "cols", 0, 0)
    return finish(near, far, product, bands, math.sqrt(rows_here * row_devices))


def solution(mesh):
    return jax.shard_map(
        shards,
        mesh=mesh,
        in_specs=(P(None, "rows"), P(None, "cols"), P("cols"), P("cols"), P("cols", None)),
        out_specs=(P("rows", None), P(("cols", "rows"), None)),
        check_vma=False,
    )
```
